128 devices in a mesh: dp: 4 (over x), clus: 32 (over y, z, core).
Axes of the slice: x: 4, y: 4, z: 4, core: 2. Of those that a mesh axis runs over, the one named last changes fastest.
Arguments:
- embeddings: bfloat16 [65536, 1024], P(('dp', 'clus')), may hold values from -8 to 8
- parents: int32 [65536, 8], P(('dp', 'clus')), may hold values from 0 to 255, all different within a row; in each aligned block of 512 rows (0 to 511, 512 to 1023, ...) at most 32 rows name the same one
- children: int32 [65536, 8], P(('dp', 'clus')), may hold values from 0 to 1
- temper: float32 [256], P('clus'), may hold values from 0.5 to 2
- level_two: bfloat16 [32768, 1024], P('clus'), may hold values from -2 to 2
- level_three: bfloat16 [65536, 1024], P('clus'), may hold values from -0.1875 to 0.1875
Outputs:
- soft_codes: bfloat16 [65536, 1024], P(('dp', 'clus'))
- candidate_scores: float32 [65536, 1024], P(('dp', 'clus'))
- new_centroids: float32 [32768, 1024], P('clus')
- cluster_mass: float32 [32768], P('clus')
The draws below stay inside these ranges and needn't reach their ends.
Inputs may be any that keep to these rules, and one draw needn't show every extreme that they name: `parents`: each row names 8 different blocks. Among the rows of one device no block is named by more than 32 rows, and in every draw some block is named by exactly 32 rows of one device.
All inputs are finite; a program needn't handle non-finite values.
Results may differ from the reference program's by a relative error of at most 0.0045.
Values may be sent and summed in bfloat16 or wider, within the bound.
A program may use at most 192 MiB of HBM per device.

```python
import math
import jax
import jax.numpy as jnp
import numpy as np
from jax import lax

D = 1024
BLOCK = 128
PARENTS = 8
CHILDREN = 2
ROW_DEV = 512
BLOCKS = 256
ROWS = 65536
MOST = 32
N_DP = 4
N_CLUS = 32


def draw_embeddings(key, part):
    first = jax.random.fold_in(jax.random.fold_in(key, 11), 0)
    base = jax.random.normal(first, (ROWS, D), jnp.float32)
    values = jnp.clip(base, -6.0, 6.0)
    return values.astype(jnp.bfloat16)


def draw_level_two(key, part):
    first = jax.random.fold_in(jax.random.fold_in(key, 23), 0)
    base = jax.random.normal(first, (BLOCKS * BLOCK, D), jnp.float32) * D ** (-0.5)
    base = jnp.clip(base, -6.0 * D ** (-0.5), 6.0 * D ** (-0.5))
    values = base
    return values.astype(jnp.bfloat16)


def place_ends(entries, own_key, smallest, largest):
    spot = [jax.random.randint(jax.random.fold_in(own_key, axis), (), 0, length) for axis, length in enumerate(entries.shape)]
    main_axis = entries.shape.index(max(entries.shape))
    neighbour = spot[:main_axis] + [(spot[main_axis] + 1) % entries.shape[main_axis]] + spot[main_axis + 1:]
    return entries.at[tuple(spot)].set(smallest).at[tuple(neighbour)].set(largest)


def shard_levels(key, shape, cuts, smallest, largest):
    loudness, own = 1.0, jax.random.fold_in(key, 6)
    for dim, shards_of in cuts:
        heights = jnp.exp(jax.random.uniform(jax.random.fold_in(own, dim), (shards_of,), jnp.float32, smallest / len(cuts), largest / len(cuts)))
        loudness = loudness * jnp.repeat(heights, shape[dim] // shards_of).reshape([-1 if axis == dim else 1 for axis in range(len(shape))])
    return loudness


def assign_block(stream_key, own, number, rows, amount, top, limit, slope):
    sequence = jax.random.permutation(stream_key, amount)
    heavy_load, ordinary = portions_of(amount, rows * top, limit, slope, True), portions_of(amount, rows * top, limit, slope, False)
    places = jnp.arange(amount)

    def named(tallies, turn):
        used = int((tallies > 0).sum())
        fixed = max(1, used // 4)
        moved = fixed + (places - fixed + turn * (used - fixed)) % max(1, amount - fixed)
        return jnp.zeros((amount,), jnp.int32).at[sequence[jnp.where(places < fixed, places, moved)]].set(jnp.asarray(tallies, jnp.int32))

    tallies = jnp.where(number % 4 == 0, named(heavy_load, number // 4), named(ordinary, number - number // 4 - 1))
    mixed = jax.random.permutation(jax.random.fold_in(own, 3), amount)
    donor, taker = mixed[0:amount // 2 * 2:2], mixed[1:amount // 2 * 2:2]
    room = jnp.minimum(tallies[donor] - 1, limit - tallies[taker]) // 2
    room = jnp.where((donor == sequence[0]) | (taker == sequence[0]) | (tallies[taker] == 0), 0, jnp.maximum(room, 0))
    moved = jax.random.randint(jax.random.fold_in(own, 4), (amount // 2,), 0, 1 << 20) % (room + 1)
    tallies = tallies.at[donor].add(-moved).at[taker].add(moved)
    items = jnp.searchsorted(jnp.cumsum(tallies), jnp.arange(rows * top), side="right").astype(jnp.int32)
    grid = items.reshape(top, rows).T
    grid = grid[jax.random.permutation(jax.random.fold_in(own, 1), rows)]
    turn = jax.random.randint(jax.random.fold_in(own, 2), (rows, 1), 0, top)
    return jnp.take_along_axis(grid, (jnp.arange(top)[None, :] + turn) % top, axis=1)


def portions_of(count, total, reach, skew, full):
    loads = [(1 << 20) // math.isqrt(standing ** skew) + 1 for standing in range(1, count + 1)]
    largest = reach if full else min(reach, max(-(-total // count), total * loads[0] // sum(loads)))
    least = 1 if total - largest >= count - 1 else 0
    holding, rest = [largest] + [least] * (count - 1), total - largest - least * (count - 1)
    while rest > 0:
        candidates = [i for i in range(1, count) if holding[i] < largest] or [i for i in range(1, count) if holding[i] < reach]
        whole, remaining = sum([loads[i] for i in candidates]), rest
        for i in candidates:
            extra = min(reach - holding[i], max(1, remaining * loads[i] // whole), rest)
            holding[i] = holding[i] + extra
            rest = rest - extra
    return np.array(holding)


def scatter_about(own_key, dims, scale, most, shards=(), kind=jnp.bfloat16):
    values = scale * jax.random.normal(own_key, dims, jnp.float32)
    if shards:
        values = values * shard_levels(own_key, dims, shards, -0.22, 0.18)
    return jnp.clip(values, -most, most).astype(kind)


def setup_inputs(seed: int = 0) -> dict:
    streams_of = jax.random.split(jax.random.key(seed), 7)
    embeddings = draw_embeddings(jax.random.fold_in(streams_of[6], 71), 0)
    parents_keys = jax.random.split(jax.random.fold_in(streams_of[1], 1), ROWS // ROW_DEV)
    parents_turns = jax.random.permutation(jax.random.fold_in(streams_of[1], 3), ROWS // ROW_DEV)
    parents = jax.vmap(lambda own, number: assign_block(jax.random.fold_in(streams_of[1], 2), own, number, ROW_DEV, BLOCKS, PARENTS, MOST, 2))(parents_keys, parents_turns).reshape((ROWS, PARENTS))
    children = place_ends(jax.random.randint(streams_of[2], (ROWS, PARENTS), 0, CHILDREN), jax.random.fold_in(streams_of[2], 1), 0, CHILDREN - 1).astype(jnp.int32)
    temper = jnp.clip(jnp.exp(math.log(2.0) - 1.3862944 * jax.random.uniform(streams_of[3], (BLOCKS,), jnp.float32) ** shard_levels(streams_of[3], (BLOCKS,), ((0, 32),), -0.2, 0.2)), 0.5, 2.0)
    level_two = draw_level_two(jax.random.fold_in(streams_of[6], 71), 0)
    level_three = scatter_about(streams_of[5], (BLOCKS * CHILDREN * BLOCK, D), D ** -0.5, 0.1875, ((0, 32),))
    return {"embeddings": embeddings, "parents": parents, "children": children, "temper": temper, "level_two": level_two, "level_three": level_three}


def reference(embeddings, parents, children, temper, level_two, level_three):
    item_count = ROWS * PARENTS
    capacity = MOST * N_DP * N_CLUS
    flat_blocks = parents.reshape(-1).astype(jnp.int32)
    flat_child = children.reshape(-1).astype(jnp.int32)
    sorted_items = jnp.argsort(flat_blocks, stable=True).astype(jnp.int32)
    counts = jnp.zeros((BLOCKS,), jnp.int32).at[flat_blocks].add(1)
    starts = counts.cumsum() - counts

    def members(block_index):
        offsets = jnp.arange(capacity, dtype=jnp.int32)
        positions = jnp.minimum(starts[block_index] + offsets, item_count - 1)
        return sorted_items[positions], offsets < counts[block_index]

    def score_block(block_index):
        item_ids, is_valid = members(block_index)
        vectors = embeddings[item_ids // PARENTS].astype(jnp.float32)
        centroids = lax.dynamic_slice_in_dim(level_two, block_index * BLOCK, BLOCK, 0).astype(jnp.float32)
        scores = jnp.dot(vectors, centroids.T) * temper[block_index]
        third = lax.dynamic_slice_in_dim(level_three, block_index * CHILDREN * BLOCK, CHILDREN * BLOCK, 0)
        third = third.astype(jnp.float32).reshape(CHILDREN, BLOCK, D)
        all_children = jnp.einsum('nd,kcd->nkc', vectors, third)
        picked = jnp.take_along_axis(all_children, flat_child[item_ids][:, None, None], axis=1)[:, 0]
        return scores, picked

    block_ids = jnp.arange(BLOCKS, dtype=jnp.int32)
    score_all, deeper_all = lax.map(score_block, block_ids)
    item_all, valid_all = jax.vmap(members)(block_ids)
    target = jnp.where(valid_all, item_all, item_count).reshape(-1)
    empty = jnp.zeros((item_count + 1, BLOCK), jnp.float32)
    scores = empty.at[target].set(score_all.reshape(-1, BLOCK))[:item_count].reshape(ROWS, PARENTS * BLOCK)
    deeper = empty.at[target].set(deeper_all.reshape(-1, BLOCK))[:item_count].reshape(ROWS, PARENTS, BLOCK)
    top = jnp.max(scores, axis=1, keepdims=True)
    weights = jnp.exp(scores - top)
    total = jnp.sum(weights, axis=1, keepdims=True)
    probs = weights / total
    soft_codes = probs.astype(jnp.bfloat16)
    mass = probs.reshape(ROWS, PARENTS, BLOCK).sum(axis=2)
    candidate_scores = (PARENTS * mass[:, :, None] * deeper).reshape(ROWS, PARENTS * BLOCK)
    code_items = probs.reshape(item_count, BLOCK)

    def sum_block(block_index):
        item_ids, is_valid = members(block_index)
        codes_here = code_items[item_ids] * is_valid[:, None].astype(jnp.float32)
        vectors = embeddings[item_ids // PARENTS].astype(jnp.float32)
        return jnp.dot(codes_here.T, vectors, precision=lax.Precision.HIGHEST), jnp.sum(codes_here, axis=0)

    weighted, block_mass = lax.map(sum_block, block_ids)
    cluster_mass = block_mass.reshape(BLOCKS * BLOCK)
    new_centroids = weighted.reshape(BLOCKS * BLOCK, D) / jnp.maximum(cluster_mass, 1.0)[:, None]
    return soft_codes, candidate_scores, new_centroids, cluster_mass
```

```python
import jax
import jax.numpy as jnp
from jax import lax
from jax.experimental import pallas as pl
from jax.experimental.pallas import tpu as pltpu
from jax.sharding import PartitionSpec as P

F32, BF16, I32 = jnp.float32, jnp.bfloat16, jnp.int32
VMEM_LIMIT = 60 << 20


def strict_upper(size):
    row = lax.broadcasted_iota(I32, (size, size), 0)
    column = lax.broadcasted_iota(I32, (size, size), 1)
    return jnp.where(row < column, 1.0, 0.0).astype(BF16)


def score_kernel(first_ref, temper_ref, meta_ref, rows_ref, w_ref,
                 g_ref, e_ref, pay_ref, stat_ref, child_ref, upper_ref):
    group, parents, rows = meta_ref.shape
    blocks, depth, width = w_ref.shape
    size = width // 3
    slots = stat_ref.shape[1]
    first = first_ref[0]

    @pl.when(pl.program_id(0) == 0)
    def _():
        upper_ref[...] = strict_upper(rows)

    slot_id = lax.broadcasted_iota(I32, (slots, rows), 0).astype(F32)
    lane = lax.broadcasted_iota(I32, (slots, 128), 1)

    @pl.loop(0, group)
    def _(s):
        packed = meta_ref[s]
        block = lax.shift_right_logical(packed, 1) - first
        child = (packed & 1).astype(F32)
        hits, childs = [], []
        for b in range(blocks):
            match = block == b
            hits.append(jnp.sum(jnp.where(match, 1.0, 0.0), axis=0, keepdims=True))
            childs.append(jnp.sum(jnp.where(match, child, 0.0), axis=0, keepdims=True))
        hit = jnp.concatenate(hits, axis=0)
        rank = jnp.dot(hit.astype(BF16), upper_ref[...], preferred_element_type=F32)
        rank = jnp.where(hit > 0.0, rank, -1.0)
        selects = []
        child_lanes = jnp.zeros((slots, 128), F32)
        for b in range(blocks):
            select = slot_id == rank[b:b + 1]
            column = jnp.sum(jnp.where(select, childs[b], 0.0), axis=1, keepdims=True)
            child_lanes = jnp.where(lane == b, column, child_lanes)
            selects.append(jnp.where(select, 1.0, 0.0).astype(BF16))
        select = jnp.concatenate(selects, axis=0)
        source_rows = rows_ref[pl.ds(pl.multiple_of(s * rows, rows), rows), :]
        gathered = jnp.dot(select, source_rows, preferred_element_type=F32).astype(BF16)
        place = pl.ds(pl.multiple_of(s * slots, slots), slots)
        child_ref[place, :] = child_lanes
        for b in range(blocks):
            g_ref[b, place, :] = gathered[b * slots:(b + 1) * slots]

    wide_lane = lax.broadcasted_iota(I32, (group * slots, 128), 1)
    stats = jnp.zeros((group * slots, 128), F32)
    for b in range(blocks):
        product = jnp.dot(g_ref[b], w_ref[b], preferred_element_type=F32)
        score = product[:, :size] * temper_ref[b]
        deeper = jnp.where(
            child_ref[:, b:b + 1] > 0.5, product[:, 2 * size:], product[:, size:2 * size]
        ).astype(BF16)
        most = jnp.max(score, axis=1, keepdims=True)
        weight = jnp.exp(score - most)
        stats = jnp.where(wide_lane == b, most, stats)
        stats = jnp.where(wide_lane == 64 + b, jnp.sum(weight, axis=1, keepdims=True), stats)
        e_ref[b] = weight
        weight = weight.astype(BF16)
        for s in range(group):
            pay_ref[s, b * slots:(b + 1) * slots, :size] = weight[s * slots:(s + 1) * slots]
            pay_ref[s, b * slots:(b + 1) * slots, size:] = deeper[s * slots:(s + 1) * slots]
    for s in range(group):
        stat_ref[s] = stats[s * slots:(s + 1) * slots]


def combine_kernel(packed_ref, most_ref, sum_ref, back_ref, scale_ref, mass_ref, slot_ref,
                   rank_ref, dense_ref, part_ref):
    parents, rows = packed_ref.shape
    all_blocks, slots = most_ref.shape
    block = lax.shift_right_logical(packed_ref[...], 1)
    number = lax.broadcasted_iota(I32, (all_blocks, rows), 0)
    hit = jnp.zeros((all_blocks, rows), F32)
    for j in range(parents):
        hit = hit + jnp.where(block[j:j + 1] == number, 1.0, 0.0)
    rank = jnp.dot(hit.astype(BF16), strict_upper(rows), preferred_element_type=F32)
    rank_ref[...] = jnp.where(hit > 0.0, rank, -1.0)

    @pl.loop(0, all_blocks // 8)
    def _(i):
        here = pl.ds(pl.multiple_of(i * 8, 8), 8)
        rank = rank_ref[here, :]
        most, total = most_ref[here, :], sum_ref[here, :]
        dense_most = jnp.full((8, rows), -3e38, F32)
        dense_sum = jnp.zeros((8, rows), F32)
        for k in range(slots):
            match = rank == k
            dense_most = jnp.where(match, most[:, k:k + 1], dense_most)
            dense_sum = jnp.where(match, total[:, k:k + 1], dense_sum)
        dense_ref[here, :] = dense_most
        part_ref[here, :] = dense_sum

    rank = rank_ref[...]
    top = jnp.max(dense_ref[...], axis=0, keepdims=True)
    weight = jnp.where(rank >= 0.0, jnp.exp(dense_ref[...] - top), 0.0)
    total = jnp.sum(weight * part_ref[...], axis=0, keepdims=True)
    scale = weight / total
    dense_ref[...] = scale
    part_ref[...] = scale * part_ref[...]
    for j in range(parents):
        match = block[j:j + 1] == number
        scale_ref[j:j + 1, :] = jnp.sum(jnp.where(match, dense_ref[...], 0.0), axis=0, keepdims=True)
        mass_ref[j:j + 1, :] = jnp.sum(jnp.where(match, part_ref[...], 0.0), axis=0, keepdims=True)
        place = jnp.where(match, number.astype(F32) * slots + rank_ref[...], 0.0)
        slot_ref[j:j + 1, :] = jnp.sum(place, axis=0, keepdims=True).astype(I32)
    lane = lax.broadcasted_iota(I32, (8, slots), 1)

    @pl.loop(0, all_blocks // 8)
    def _(i):
        here = pl.ds(pl.multiple_of(i * 8, 8), 8)
        rank, scale = rank_ref[here, :], dense_ref[here, :]
        back = jnp.zeros((8, slots), F32)
        for k in range(slots):
            column = jnp.sum(jnp.where(rank == k, scale, 0.0), axis=1, keepdims=True)
            back = jnp.where(lane == k, column, back)
        back_ref[here, :] = back


def sum_kernel(scale_ref, e_ref, g_ref, weighted_ref, mass_ref):
    b = pl.program_id(0)
    lane = lax.broadcasted_iota(I32, scale_ref.shape, 1)
    scale = jnp.sum(jnp.where(lane == b, scale_ref[...], 0.0), axis=1, keepdims=True)
    codes = e_ref[0] * scale
    mass_ref[0] = jnp.sum(codes, axis=0, keepdims=True)
    weighted_ref[0] = lax.dot_general(
        codes.astype(BF16), g_ref[0], (((0,), (0,)), ((), ())), preferred_element_type=F32
    )


def spread_kernel(slot_ref, scale_ref, mass_ref, pay_ref, codes_ref, deeper_ref, wide_ref, code_ref, deep_ref):
    rows, parents = scale_ref.shape
    size = pay_ref.shape[1] // 2
    count = pay_ref.shape[0]
    chunk = min(512, count)

    @pl.loop(0, count // chunk)
    def _(i):
        here = pl.ds(pl.multiple_of(i * chunk, chunk), chunk)
        wide_ref[here, :] = pay_ref[here, :].astype(F32)

    @pl.loop(0, rows // 16)
    def _(i):
        for r in range(16):
            for j in range(parents):
                slot = slot_ref[(i * 16 + r) * parents + j]
                item = wide_ref[pl.ds(slot, 1), :]
                code_ref[r:r + 1, j * size:(j + 1) * size] = item[:, :size]
                deep_ref[r:r + 1, j * size:(j + 1) * size] = item[:, size:]
        here = pl.ds(pl.multiple_of(i * 16, 16), 16)
        scale, mass = scale_ref[here, :], mass_ref[here, :]
        for j in range(parents):
            part = slice(j * size, (j + 1) * size)
            codes_ref[here, part] = (code_ref[:, part] * scale[:, j:j + 1]).astype(BF16)
            deeper_ref[here, part] = deep_ref[:, part] * (parents * mass[:, j:j + 1])


def params():
    return pltpu.CompilerParams(vmem_limit_bytes=VMEM_LIMIT)


def whole(shape):
    return pl.BlockSpec(shape, lambda *_: (0,) * len(shape))


def body(embeddings, parents, children, temper, level_two, level_three):
    rows, depth = embeddings.shape
    count = parents.shape[1]
    blocks = temper.shape[0]
    size = level_two.shape[0] // blocks
    kinds = level_three.shape[0] // (blocks * size)
    assert kinds == 2
    shards = lax.axis_size("clus")
    own = lax.axis_index("clus")
    all_blocks = blocks * shards
    slots = 2 * rows * count // all_blocks
    group = min(8, shards)

    packed = (parents * kinds + children).T
    all_rows = lax.all_gather(embeddings, "clus", axis=0, tiled=True)
    all_packed = lax.all_gather(packed, "clus", axis=0, tiled=False)
    table = jnp.concatenate(
        [level_two.reshape(blocks, size, depth), level_three.reshape(blocks, kinds * size, depth)], axis=1
    ).transpose(0, 2, 1)
    first = (own * blocks).reshape(1).astype(I32)

    gathered, weights, pay, stats = pl.pallas_call(
        score_kernel,
        grid=(shards // group,),
        in_specs=[
            pl.BlockSpec(memory_space=pltpu.SMEM),
            pl.BlockSpec(memory_space=pltpu.SMEM),
            pl.BlockSpec((group, count, rows), lambda i: (i, 0, 0)),
            pl.BlockSpec((group * rows, depth), lambda i: (i, 0)),
            pl.BlockSpec(table.shape, lambda i: (0, 0, 0), pipeline_mode=pl.Buffered(1)),
        ],
        out_specs=[
            pl.BlockSpec((blocks, group * slots, depth), lambda i: (0, i, 0)),
            pl.BlockSpec((blocks, group * slots, size), lambda i: (0, i, 0)),
            pl.BlockSpec((group, blocks * slots, 2 * size), lambda i: (i, 0, 0)),
            pl.BlockSpec((group, slots, 128), lambda i: (i, 0, 0)),
        ],
        out_shape=[
            jax.ShapeDtypeStruct((blocks, shards * slots, depth), BF16),
            jax.ShapeDtypeStruct((blocks, shards * slots, size), F32),
            jax.ShapeDtypeStruct((shards, blocks * slots, 2 * size), BF16),
            jax.ShapeDtypeStruct((shards, slots, 128), F32),
        ],
        scratch_shapes=[pltpu.VMEM((group * slots, 128), F32), pltpu.VMEM((rows, rows), BF16)],
        compiler_params=params(),
    )(first, temper, all_packed, all_rows, table)

    returned = lax.all_to_all(pay, "clus", split_axis=0, concat_axis=0, tiled=True)
    kept = jnp.concatenate([stats[:, :, :blocks], stats[:, :, 64:64 + blocks]], axis=2)
    kept = lax.all_to_all(kept, "clus", split_axis=0, concat_axis=0, tiled=True)
    kept = kept.transpose(0, 2, 1)
    most = kept[:, :blocks].reshape(all_blocks, slots)
    sums = kept[:, blocks:].reshape(all_blocks, slots)

    back, scale, mass, place = pl.pallas_call(
        combine_kernel,
        out_shape=[
            jax.ShapeDtypeStruct((all_blocks, slots), F32),
            jax.ShapeDtypeStruct((count, rows), F32),
            jax.ShapeDtypeStruct((count, rows), F32),
            jax.ShapeDtypeStruct((count, rows), I32),
        ],
        scratch_shapes=[pltpu.VMEM((all_blocks, rows), F32)] * 3,
        compiler_params=params(),
    )(packed, most, sums)

    scales = lax.all_to_all(
        back.reshape(shards, blocks, slots), "clus", split_axis=0, concat_axis=0, tiled=True
    )
    scales = scales.transpose(0, 2, 1).reshape(shards * slots, blocks)

    partial, partial_mass = pl.pallas_call(
        sum_kernel,
        grid=(blocks,),
        in_specs=[
            whole(scales.shape),
            pl.BlockSpec((1, shards * slots, size), lambda i: (i, 0, 0)),
            pl.BlockSpec((1, shards * slots, depth), lambda i: (i, 0, 0)),
        ],
        out_specs=[
            pl.BlockSpec((1, size, depth), lambda i: (i, 0, 0)),
            pl.BlockSpec((1, 1, size), lambda i: (i, 0, 0)),
        ],
        out_shape=[
            jax.ShapeDtypeStruct((blocks, size, depth), F32),
            jax.ShapeDtypeStruct((blocks, 1, size), F32),
        ],
        compiler_params=params(),
    )(scales, weights, gathered)

    soft_codes, candidate_scores = pl.pallas_call(
        spread_kernel,
        in_specs=[
            pl.BlockSpec(memory_space=pltpu.SMEM),
            whole((rows, count)),
            whole((rows, count)),
            whole((all_blocks * slots, 2 * size)),
        ],
        out_shape=[
            jax.ShapeDtypeStruct((rows, count * size), BF16),
            jax.ShapeDtypeStruct((rows, count * size), F32),
        ],
        scratch_shapes=[
            pltpu.VMEM((all_blocks * slots, 2 * size), F32),
            pltpu.VMEM((16, count * size), F32),
            pltpu.VMEM((16, count * size), F32),
        ],
        compiler_params=params(),
    )(place.T.reshape(-1), scale.T, mass.T, returned.reshape(all_blocks * slots, 2 * size))

    weighted, cluster_mass = lax.psum((partial, partial_mass), "dp")
    cluster_mass = cluster_mass.reshape(blocks * size)
    new_centroids = weighted.reshape(blocks * size, depth) / jnp.maximum(cluster_mass, 1.0)[:, None]
    return soft_codes, candidate_scores, new_centroids, cluster_mass


def solution(mesh):
    rows = P(("dp", "clus"), None)
    return jax.shard_map(
        body,
        mesh=mesh,
        in_specs=(rows, rows, rows, P("clus"), P("clus", None), P("clus", None)),
        out_specs=(rows, rows, P("clus", None), P("clus")),
        check_vma=False,
    )
```

```python
import jax
import jax.numpy as jnp
from jax import lax
from jax.experimental import pallas as pl
from jax.experimental.pallas import tpu as pltpu
from jax.sharding import PartitionSpec as P

F32, BF16, I32 = jnp.float32, jnp.bfloat16, jnp.int32
MESH = pl.DeviceIdType.MESH
VMEM_LIMIT = 60 << 20

ORDER = (
    (0, 0), (1, 0), (3, 0), (0, 1), (0, 3), (2, 0), (0, 2), (1, 1),
    (3, 3), (3, 1), (1, 3), (2, 1), (2, 3), (1, 2), (3, 2), (2, 2),
)
WAVES = (0, 12, 24, 32)
RING = (0, 1, 3, 2)


def packed_table(values):
    word = sum(v << (2 * i) for i, v in enumerate(values))
    return word - (1 << 32) if word >= 1 << 31 else word


TABLE_Y = packed_table([o[0] for o in ORDER])
TABLE_Z = packed_table([o[1] for o in ORDER])


def entry(table, index):
    return lax.shift_right_logical(jnp.int32(table), jnp.int32(2) * index) % 4


def strict_upper(size):
    row = lax.broadcasted_iota(I32, (size, size), 0)
    column = lax.broadcasted_iota(I32, (size, size), 1)
    return jnp.where(row < column, 1.0, 0.0).astype(BF16)


def three(x):
    high = x.astype(BF16)
    rest = x - high.astype(F32)
    middle = rest.astype(BF16)
    low = (rest - middle.astype(F32)).astype(BF16)
    return high, middle, low


def fused_kernel(
    temper_ref, ext_ref, packed_ref, two_ref, three_ref,
    buf_ref, ret_ref, scale_ref, mass_ref, slot_ref, fin_ref, total_ref,
    rowbuf, w2, w3, g, et, pay, child, upper, stats, stat_out, stat_in, onehot, item_rank, back_out, back_in,
    sc, part, relay_in, near_in, own, mass_all, mass_send, column_scr,
    load_sem, w_sem, local_sem, ring_send, ring_recv, sib_send, sib_recv, pay_send, pay_recv,
    stat_send, stat_recv, back_send, back_recv, dp_send, dp_recv,
):
    parents, rows = packed_ref.shape
    total_rows, depth = ext_ref.shape
    slots = 32
    blocks = temper_ref.shape[0]
    size = w2.shape[0] // blocks
    shards = buf_ref.shape[0]
    all_blocks = blocks * shards
    dp = lax.axis_index("dp")
    me = lax.axis_index("clus")
    core = me % 2
    z = (me // 2) % 4
    y = me // 8
    sibling = me + 1 - 2 * core

    def at(dy, dz, flip=0):
        return (((y + dy) % 4) * 4 + (z + dz) % 4) * 2 + (core + flip) % 2

    def source(p):
        q = p // 2
        return at(entry(TABLE_Y, q), entry(TABLE_Z, q), p % 2)

    def holder(p):
        q = p // 2
        return at(4 - entry(TABLE_Y, q), 4 - entry(TABLE_Z, q), p % 2)

    barrier = pltpu.get_barrier_semaphore()

    @pl.loop(1, shards)
    def _(d):
        pl.semaphore_signal(barrier, inc=1, device_id=(dp, (me + d) % shards), device_id_type=MESH)

    for d in (1, 2, 3):
        pl.semaphore_signal(barrier, inc=1, device_id=((dp + d) % 4, me), device_id_type=MESH)
    pl.semaphore_wait(barrier, shards - 1 + 3)

    quarter = rows // 4
    ids = total_rows - rows
    piece = {
        "A": (0, ids + 2 * quarter), "A0": (0, ids + quarter), "A1": (ids + quarter, quarter),
        "B": (ids + 2 * quarter, 2 * quarter), "B0": (ids + 2 * quarter, quarter), "B1": (ids + 3 * quarter, quarter),
    }

    def part_of(ref, name):
        start, length = piece[name]
        return ref.at[pl.ds(start, length), :]

    def chip(half, first, second):
        return (first, second) if half == "A" else (second, first)

    def ring(half, k, offset, name, step):
        index = (0 if half == "A" else 20) + k
        block = at(*offset)
        mine = ext_ref if offset == (0, 0) else buf_ref.at[block]
        return pltpu.make_async_remote_copy(
            src_ref=part_of(mine, name), dst_ref=part_of(buf_ref.at[block], name),
            send_sem=ring_send.at[index], recv_sem=ring_recv.at[index],
            device_id=(dp, at(*step)), device_id_type=MESH,
        )

    def arrival(half, k, offset, name):
        index = (0 if half == "A" else 20) + k
        block = at(*offset)
        return pltpu.make_async_remote_copy(
            src_ref=part_of(buf_ref.at[block], name), dst_ref=part_of(buf_ref.at[block], name),
            send_sem=ring_send.at[index], recv_sem=ring_recv.at[index],
            device_id=(dp, at(1, 0)), device_id_type=MESH,
        )

    sent = []

    def go(copy):
        copy.start()
        sent.append(copy)

    def share(half, offset):
        index = (0 if half == "A" else 16) + ORDER.index(offset)
        block = at(*offset)
        mine = ext_ref if offset == (0, 0) else buf_ref.at[block]
        go(pltpu.make_async_remote_copy(
            src_ref=part_of(mine, half), dst_ref=part_of(buf_ref.at[block], half),
            send_sem=sib_send.at[index], recv_sem=sib_recv.at[index],
            device_id=(dp, sibling), device_id_type=MESH,
        ))

    def shared(half, q):
        index = (0 if half == "A" else 16) + q
        block = at(*ORDER[q], 1)
        pltpu.make_async_remote_copy(
            src_ref=part_of(buf_ref.at[block], half), dst_ref=part_of(buf_ref.at[block], half),
            send_sem=sib_send.at[index], recv_sem=sib_recv.at[index],
            device_id=(dp, sibling), device_id_type=MESH,
        ).wait_recv()

    def first_axis(half, step):
        return chip(half, step, 0)

    def second_axis(half, step):
        return chip(half, 0, step)

    def enter_second(half, i):
        block = chip(half, RING[i], 0)
        go(ring(half, 4 + 4 * i, block, half, second_axis(half, 1)))
        go(ring(half, 5 + 4 * i, block, half, second_axis(half, 3)))

    def first_near(half):
        arrival(half, 1, chip(half, 1, 0), half).wait_recv()
        go(ring(half, 3, chip(half, 1, 0), half + "1", first_axis(half, 3)))
        arrival(half, 0, chip(half, 3, 0), half).wait_recv()
        go(ring(half, 2, chip(half, 3, 0), half + "0", first_axis(half, 1)))
        enter_second(half, 1)
        enter_second(half, 2)
        share(half, chip(half, 1, 0))
        share(half, chip(half, 3, 0))

    def first_far(half):
        arrival(half, 2, chip(half, 2, 0), half + "0").wait_recv()
        arrival(half, 3, chip(half, 2, 0), half + "1").wait_recv()
        enter_second(half, 3)
        share(half, chip(half, 2, 0))

    def second_near(half, i):
        o = RING[i]
        arrival(half, 5 + 4 * i, chip(half, o, 1), half).wait_recv()
        go(ring(half, 7 + 4 * i, chip(half, o, 1), half + "1", second_axis(half, 3)))
        arrival(half, 4 + 4 * i, chip(half, o, 3), half).wait_recv()
        go(ring(half, 6 + 4 * i, chip(half, o, 3), half + "0", second_axis(half, 1)))
        share(half, chip(half, o, 1))
        share(half, chip(half, o, 3))

    def second_far(half, i):
        o = RING[i]
        arrival(half, 6 + 4 * i, chip(half, o, 2), half + "0").wait_recv()
        arrival(half, 7 + 4 * i, chip(half, o, 2), half + "1").wait_recv()
        share(half, chip(half, o, 2))

    def load(p):
        return pltpu.make_async_copy(buf_ref.at[source(p)], rowbuf.at[p % 2], load_sem.at[p % 2])

    first_block = (me * blocks).astype(F32)

    def gather(low, high):
        for q in range(low // 2, high // 2):
            shared("A", q)
            shared("B", q)
        load(low).start()
        slot_id = lax.broadcasted_iota(I32, (slots, rows), 0).astype(F32)
        lane = lax.broadcasted_iota(I32, (slots, 128), 1)

        @pl.loop(low, high)
        def _(p):
            load(p).wait()

            @pl.when(p + 1 < high)
            def _():
                load(p + 1).start()

            meta = rowbuf[p % 2, 0:2 * parents, 0:rows].astype(F32)
            block = meta[:parents] - first_block
            kind = meta[parents:]
            hits, kinds = [], []
            for b in range(blocks):
                match = block == float(b)
                hits.append(jnp.sum(jnp.where(match, 1.0, 0.0), axis=0, keepdims=True))
                kinds.append(jnp.sum(jnp.where(match, kind, 0.0), axis=0, keepdims=True))
            hit = jnp.concatenate(hits, axis=0)
            rank = jnp.dot(hit.astype(BF16), upper[...], preferred_element_type=F32)
            rank = jnp.where(hit > 0.0, rank, -1.0)
            selects = []
            child_lanes = jnp.zeros((slots, 128), F32)
            for b in range(blocks):
                select = slot_id == rank[b:b + 1]
                column = jnp.sum(jnp.where(select, kinds[b], 0.0), axis=1, keepdims=True)
                child_lanes = jnp.where(lane == b, column, child_lanes)
                selects.append(jnp.where(select, 1.0, 0.0).astype(BF16))
            select = jnp.concatenate(selects, axis=0)
            picked = jnp.dot(
                select, rowbuf[p % 2, ids:total_rows, :], preferred_element_type=F32
            ).astype(BF16)
            place = pl.ds(pl.multiple_of(p * slots, slots), slots)
            child[place, :] = child_lanes
            for b in range(blocks):
                g[b, place, :] = picked[b * slots:(b + 1) * slots]

    contract_last = (((1,), (1,)), ((), ()))

    def score(wave, low, high):
        start, count = WAVES[wave] * slots, (WAVES[wave + 1] - WAVES[wave]) * slots
        here = slice(start, start + count)
        lane = lax.broadcasted_iota(I32, (count, 128), 1)

        @pl.loop(low, high)
        def _(b):
            x = g[b, here, :]
            near = lax.dot_general(
                x, w2[pl.ds(pl.multiple_of(b * size, size), size), :], contract_last, preferred_element_type=F32
            )
            far = lax.dot_general(
                x, w3[pl.ds(pl.multiple_of(b * 2 * size, 2 * size), 2 * size), :], contract_last,
                preferred_element_type=F32,
            )
            value = near * temper_ref[b]
            which = jnp.sum(jnp.where(lane == b, child[here, :], 0.0), axis=1, keepdims=True)
            deeper = jnp.where(which > 0.5, far[:, size:], far[:, :size]).astype(BF16)
            most = jnp.max(value, axis=1, keepdims=True)
            weight = jnp.exp(value - most)
            amount = jnp.sum(weight, axis=1, keepdims=True)
            old = stats[here, :]
            stats[here, :] = jnp.where(lane == b, most, jnp.where(lane == b + blocks, amount, old))
            et[b, :, here] = weight.T
            weight = weight.astype(BF16)
            place = pl.ds(pl.multiple_of(b * slots, slots), slots)
            for i in range(count // slots):
                pay[WAVES[wave] + i, place, 0:size] = weight[i * slots:(i + 1) * slots]
                pay[WAVES[wave] + i, place, size:2 * size] = deeper[i * slots:(i + 1) * slots]

    def each(low, high, action):
        @pl.loop(max(low, 1), high)
        def _(p):
            action(p)

    def stat_copy(p, index, device):
        return pltpu.make_async_remote_copy(
            src_ref=stat_out.at[p], dst_ref=stat_in.at[index], send_sem=stat_send.at[p], recv_sem=stat_recv.at[p],
            device_id=(dp, device), device_id_type=MESH,
        )

    def send_stats(wave):
        low, high = WAVES[wave], WAVES[wave + 1]
        for t in range(low // 4, high // 4):
            flipped = stats[t * 128:(t + 1) * 128, :].T[0:2 * blocks, :]
            for s in range(4):
                moved = flipped if s == 0 else pltpu.roll(flipped, 128 - s * slots, 1)
                stat_out[t * 4 + s] = moved
        if low == 0:
            stat_in[me] = stat_out[0]
        each(low, high, lambda p: stat_copy(p, me, source(p)).start())

    def pay_copy(p, index, device):
        return pltpu.make_async_remote_copy(
            src_ref=pay.at[p], dst_ref=ret_ref.at[index], send_sem=pay_send.at[p], recv_sem=pay_recv.at[p],
            device_id=(dp, device), device_id_type=MESH,
        )

    def send_pay(low, high):
        each(low, high, lambda p: pay_copy(p, me, source(p)).start())

    def back_copy(p, index, device):
        return pltpu.make_async_remote_copy(
            src_ref=back_out.at[index], dst_ref=back_in.at[p], send_sem=back_send.at[p], recv_sem=back_recv.at[p],
            device_id=(dp, device), device_id_type=MESH,
        )

    for half, step in (("A", 1), ("B", 1)):
        go(ring(half, 0, (0, 0), half, first_axis(half, 1)))
        go(ring(half, 1, (0, 0), half, first_axis(half, 3)))
    enter_second("A", 0)
    enter_second("B", 0)
    share("A", (0, 0))
    share("B", (0, 0))
    in_two = pltpu.make_async_copy(two_ref, w2, w_sem.at[0])
    in_three = pltpu.make_async_copy(three_ref, w3, w_sem.at[1])
    in_two.start()
    in_three.start()
    own_in = pltpu.make_async_copy(ext_ref, rowbuf.at[0], local_sem.at[0])
    own_in.start()
    upper[...] = strict_upper(rows)
    stats[...] = jnp.zeros_like(stats)
    back_out[...] = jnp.zeros_like(back_out)
    own_in.wait()
    own_out = pltpu.make_async_copy(rowbuf.at[0], buf_ref.at[me], local_sem.at[1])
    own_out.start()

    named = lax.shift_right_logical(packed_ref[...], 1)
    number = lax.broadcasted_iota(I32, (all_blocks, rows), 0)
    hit = jnp.zeros((all_blocks, rows), F32)
    for j in range(parents):
        one = jnp.where(named[j:j + 1] == number, 1.0, 0.0)
        hit = hit + one
        onehot[j] = one.astype(BF16)
    own_rank = jnp.dot(hit.astype(BF16), upper[...], preferred_element_type=F32)
    for j in range(parents):
        item_rank[j:j + 1, :] = jnp.sum(onehot[j].astype(F32) * own_rank, axis=0, keepdims=True)
    slot_ref[...] = named * slots + item_rank[...].astype(I32)
    own_out.wait()

    first_near("A")
    first_near("B")
    gather(0, 2)
    second_near("A", 0)
    second_near("B", 0)
    first_far("A")
    first_far("B")
    gather(2, 6)
    second_far("A", 0)
    second_far("B", 0)
    second_near("A", 1)
    second_near("B", 1)
    gather(6, 12)
    in_two.wait()
    in_three.wait()
    second_near("A", 2)
    second_near("B", 2)
    score(0, 0, blocks)
    second_far("A", 1)
    second_far("B", 1)
    send_stats(0)
    gather(12, 18)
    second_far("A", 2)
    second_far("B", 2)
    gather(18, 22)
    second_near("A", 3)
    second_near("B", 3)
    gather(22, 24)
    score(1, 0, blocks)
    send_stats(1)
    second_far("A", 3)
    second_far("B", 3)
    send_pay(0, PAY_CUTS[0])
    gather(24, 32)
    score(2, 0, blocks)
    send_stats(2)
    send_pay(PAY_CUTS[0], PAY_CUTS[1])
    own_pay = pltpu.make_async_copy(pay.at[0], ret_ref.at[me], local_sem.at[0])
    own_pay.start()

    each(0, shards, lambda p: stat_copy(p, holder(p), source(p)).wait_recv())
    table = jnp.concatenate([stat_in[o, 0:blocks, :] for o in range(shards)], axis=0)
    table_sum = jnp.concatenate([stat_in[o, blocks:2 * blocks, :] for o in range(shards)], axis=0)
    both = jnp.concatenate([table.T[0:slots], table_sum.T[0:slots]], axis=0)
    stack = jnp.concatenate(three(both), axis=0)
    slot_row = lax.broadcasted_iota(I32, (slots, rows), 0).astype(F32)
    mosts, amounts = [], []
    for j in range(parents):
        found = jnp.dot(stack, onehot[j], preferred_element_type=F32)
        found = (found[0:2 * slots] + found[2 * slots:4 * slots]) + found[4 * slots:6 * slots]
        pick = slot_row == item_rank[j:j + 1, :]
        mosts.append(jnp.sum(jnp.where(pick, found[0:slots], 0.0), axis=0, keepdims=True))
        amounts.append(jnp.sum(jnp.where(pick, found[slots:], 0.0), axis=0, keepdims=True))
    most = jnp.concatenate(mosts, axis=0)
    amount = jnp.concatenate(amounts, axis=0)
    weight = jnp.exp(most - jnp.max(most, axis=0, keepdims=True))
    scale = weight / jnp.sum(weight * amount, axis=0, keepdims=True)
    scale_ref[...] = scale
    mass_ref[...] = scale * amount
    back = jnp.zeros((all_blocks, 4 * slots), F32)
    for j in range(parents):
        pick = slot_row == item_rank[j:j + 1, :]
        spread = jnp.where(pick, scale[j:j + 1, :], 0.0)
        pad = jnp.zeros((slots, rows), BF16)
        stacked = jnp.concatenate(three(spread) + (pad,), axis=0)
        back = back + lax.dot_general(onehot[j], stacked, contract_last, preferred_element_type=F32)
    back = (back + pltpu.roll(back, 3 * slots, 1)) + pltpu.roll(back, 2 * slots, 1)
    for o in range(shards):
        back_out[o] = back[o * blocks:(o + 1) * blocks, :]
    back_in[0] = back_out[me]
    each(0, shards, lambda p: back_copy(p, holder(p), holder(p)).start())
    send_pay(PAY_CUTS[1], shards)
    each(0, shards, lambda p: back_copy(p, holder(p), holder(p)).wait_recv())
    lane8 = lax.broadcasted_iota(I32, (blocks, 128), 1)
    for t in range(shards // 4):
        joined = back_in[4 * t]
        for s in range(1, 4):
            joined = jnp.where(lane8 >= s * slots, pltpu.roll(back_in[4 * t + s], s * slots, 1), joined)
        sc[:, t * 128:(t + 1) * 128] = joined

    def sums(b):
        codes = et[b] * sc[pl.ds(b, 1), :]
        high = codes.astype(BF16)
        low = (codes - high.astype(F32)).astype(BF16)
        product = jnp.dot(jnp.concatenate([high, low], axis=0), g[b], preferred_element_type=F32)
        return product[:size] + product[size:], jnp.sum(codes, axis=1, keepdims=True)

    lane128 = lax.broadcasted_iota(I32, (size, 128), 1)
    column_scr[...] = jnp.zeros_like(column_scr)

    @pl.loop(0, blocks)
    def _(i):
        b = (2 * ((dp + 2) % 4) + i) % blocks
        value, column = sums(b)
        part[b] = value
        column_scr[...] = jnp.where(lane128 == b, column, column_scr[...])

    def dp_copy(index, source_ref, target_ref, step):
        return pltpu.make_async_remote_copy(
            src_ref=source_ref, dst_ref=target_ref, send_sem=dp_send.at[index], recv_sem=dp_recv.at[index],
            device_id=((dp + step) % 4, me), device_id_type=MESH,
        )

    right, left, across = (dp + 1) % 4, (dp + 3) % 4, (dp + 2) % 4
    mass_send[...] = column_scr[...].T[0:blocks, :]
    mass_all[dp] = mass_send[...]
    mass_copies = [dp_copy(8 + d, mass_send, mass_all.at[dp], d) for d in (1, 2, 3)]
    for copy in mass_copies:
        copy.start()
    half_part = near_in
    own[0] = part[2 * across].astype(BF16)
    own[1] = part[2 * across + 1].astype(BF16)
    relay = [dp_copy(0, own.at[0], relay_in.at[0], 1), dp_copy(1, own.at[1], relay_in.at[1], 3)]
    for copy in relay:
        copy.start()
    own[3] = part[2 * right + 1].astype(BF16)
    own[4] = part[2 * left].astype(BF16)
    near = [
        dp_copy(2, own.at[2], half_part.at[0], 1), dp_copy(3, own.at[3], half_part.at[1], 1),
        dp_copy(4, own.at[4], half_part.at[2], 3), dp_copy(5, own.at[5], half_part.at[3], 3),
    ]
    near[1].start()
    near[2].start()
    relay[0].wait_recv()
    own[2] = (part[2 * right] + relay_in[0].astype(F32)).astype(BF16)
    near[0].start()
    relay[1].wait_recv()
    own[5] = (part[2 * left + 1] + relay_in[1].astype(F32)).astype(BF16)
    near[3].start()
    for copy in mass_copies:
        copy.wait_recv()
    all_mass = ((mass_all[0] + mass_all[1]) + mass_all[2]) + mass_all[3]
    total_ref[...] = all_mass
    spare = jnp.zeros((128 - blocks, 128), F32)
    column_scr[...] = jnp.maximum(jnp.concatenate([all_mass, spare], axis=0), 1.0).T
    for copy in near:
        copy.wait_recv()
    for i in range(2):
        b = 2 * dp + i
        column = jnp.sum(jnp.where(lane128 == b, column_scr[...], 0.0), axis=1, keepdims=True)
        value = part[b] + (half_part[i].astype(F32) + half_part[2 + i].astype(F32))
        own[6 + i] = (value / column).astype(BF16)
    ready = [
        dp_copy(12, own.at[6], fin_ref.at[2 * dp], 1), dp_copy(13, own.at[7], fin_ref.at[2 * dp + 1], 3),
        dp_copy(14, own.at[7], fin_ref.at[2 * dp + 1], 1), dp_copy(15, own.at[6], fin_ref.at[2 * dp], 3),
    ]
    for copy in ready:
        copy.start()
    own_fin = [pltpu.make_async_copy(own.at[6 + i], fin_ref.at[2 * dp + i], local_sem.at[2 + i]) for i in range(2)]
    for copy in own_fin:
        copy.start()
    dp_copy(12, own.at[6], fin_ref.at[2 * left], 1).wait_recv()
    onward = [dp_copy(6, fin_ref.at[2 * left], fin_ref.at[2 * left], 1)]
    onward[0].start()
    dp_copy(13, own.at[7], fin_ref.at[2 * right + 1], 3).wait_recv()
    onward.append(dp_copy(7, fin_ref.at[2 * right + 1], fin_ref.at[2 * right + 1], 3))
    onward[1].start()
    dp_copy(14, own.at[7], fin_ref.at[2 * left + 1], 1).wait_recv()
    dp_copy(15, own.at[6], fin_ref.at[2 * right], 3).wait_recv()
    dp_copy(6, own.at[6], fin_ref.at[2 * across], 1).wait_recv()
    dp_copy(7, own.at[7], fin_ref.at[2 * across + 1], 3).wait_recv()

    each(0, shards, lambda p: pay_copy(p, holder(p), source(p)).wait_recv())
    for copy in sent + mass_copies + relay + near + ready + onward:
        copy.wait_send()
    each(0, shards, lambda p: pay_copy(p, me, source(p)).wait_send())
    each(0, shards, lambda p: stat_copy(p, me, source(p)).wait_send())
    each(0, shards, lambda p: back_copy(p, holder(p), holder(p)).wait_send())
    own_pay.wait()
    for copy in own_fin:
        copy.wait()


PAY_CUTS = (8, 16)


def spread_kernel(slot_ref, scale_ref, mass_ref, pay_ref, codes_ref, deeper_ref, wide_ref, code_ref, deep_ref):
    rows, parents = scale_ref.shape
    size = pay_ref.shape[1] // 2
    count = pay_ref.shape[0]
    chunk = min(512, count)

    @pl.loop(0, count // chunk)
    def _(i):
        here = pl.ds(pl.multiple_of(i * chunk, chunk), chunk)
        wide_ref[here, :] = pay_ref[here, :].astype(F32)

    @pl.loop(0, rows // 16)
    def _(i):
        for r in range(16):
            for j in range(parents):
                slot = slot_ref[(i * 16 + r) * parents + j]
                item = wide_ref[pl.ds(slot, 1), :]
                code_ref[r:r + 1, j * size:(j + 1) * size] = item[:, :size]
                deep_ref[r:r + 1, j * size:(j + 1) * size] = item[:, size:]
        here = pl.ds(pl.multiple_of(i * 16, 16), 16)
        scale, mass = scale_ref[here, :], mass_ref[here, :]
        for j in range(parents):
            part = slice(j * size, (j + 1) * size)
            codes_ref[here, part] = (code_ref[:, part] * scale[:, j:j + 1]).astype(BF16)
            deeper_ref[here, part] = deep_ref[:, part] * (parents * mass[:, j:j + 1])


def params():
    return pltpu.CompilerParams(vmem_limit_bytes=VMEM_LIMIT)


def whole(shape):
    return pl.BlockSpec(shape, lambda *_: (0,) * len(shape))


def body(embeddings, parents, children, temper, level_two, level_three):
    rows, depth = embeddings.shape
    count = parents.shape[1]
    blocks = temper.shape[0]
    size = level_two.shape[0] // blocks
    kinds = level_three.shape[0] // (blocks * size)
    shards = lax.axis_size("clus")
    all_blocks = blocks * shards
    slots = 2 * rows * count // all_blocks
    assert kinds == 2 and shards == 32 and slots == 32 and blocks == 8 and lax.axis_size("dp") == 4

    packed = (parents * kinds + children).T
    ids = jnp.concatenate([parents.T, children.T], axis=0).astype(BF16)
    ids = jnp.pad(ids, ((0, 0), (0, depth - rows)))
    extended = jnp.concatenate([ids, embeddings], axis=0)
    total_rows = extended.shape[0]
    anywhere = pl.BlockSpec(memory_space=pl.ANY)
    vmem = pl.BlockSpec(memory_space=pltpu.VMEM)
    dma = pltpu.SemaphoreType.DMA

    _, returned, scale, mass, place, sums, cluster_mass = pl.pallas_call(
        fused_kernel,
        in_specs=[pl.BlockSpec(memory_space=pltpu.SMEM), anywhere, vmem, anywhere, anywhere],
        out_specs=[anywhere, anywhere, vmem, vmem, vmem, anywhere, vmem],
        out_shape=[
            jax.ShapeDtypeStruct((shards, total_rows, depth), BF16),
            jax.ShapeDtypeStruct((shards, blocks * slots, 2 * size), BF16),
            jax.ShapeDtypeStruct((count, rows), F32),
            jax.ShapeDtypeStruct((count, rows), F32),
            jax.ShapeDtypeStruct((count, rows), I32),
            jax.ShapeDtypeStruct((blocks, size, depth), BF16),
            jax.ShapeDtypeStruct((blocks, size), F32),
        ],
        scratch_shapes=[
            pltpu.VMEM((2, total_rows, depth), BF16),
            pltpu.VMEM(level_two.shape, BF16),
            pltpu.VMEM(level_three.shape, BF16),
            pltpu.VMEM((blocks, shards * slots, depth), BF16),
            pltpu.VMEM((blocks, size, shards * slots), F32),
            pltpu.VMEM((shards, blocks * slots, 2 * size), BF16),
            pltpu.VMEM((shards * slots, 128), F32),
            pltpu.VMEM((rows, rows), BF16),
            pltpu.VMEM((shards * slots, 128), F32),
            pltpu.VMEM((shards, 2 * blocks, 128), F32),
            pltpu.VMEM((shards, 2 * blocks, 128), F32),
            pltpu.VMEM((count, all_blocks, rows), BF16),
            pltpu.VMEM((count, rows), F32),
            pltpu.VMEM((shards, blocks, 128), F32),
            pltpu.VMEM((shards, blocks, 128), F32),
            pltpu.VMEM((blocks, shards * slots), F32),
            pltpu.VMEM((blocks, size, depth), F32),
            pltpu.VMEM((2, size, depth), BF16),
            pltpu.VMEM((4, size, depth), BF16),
            pltpu.VMEM((8, size, depth), BF16),
            pltpu.VMEM((4, blocks, 128), F32),
            pltpu.VMEM((blocks, 128), F32),
            pltpu.VMEM((size, 128), F32),
            dma((2,)), dma((2,)), dma((4,)), dma((40,)), dma((40,)), dma((32,)), dma((32,)),
            dma((shards,)), dma((shards,)), dma((shards,)), dma((shards,)), dma((shards,)), dma((shards,)),
            dma((16,)), dma((16,)),
        ],
        compiler_params=pltpu.CompilerParams(
            vmem_limit_bytes=VMEM_LIMIT, collective_id=0, has_side_effects=True
        ),
    )(temper, extended, packed, level_two, level_three)

    soft_codes, candidate_scores = pl.pallas_call(
        spread_kernel,
        in_specs=[
            pl.BlockSpec(memory_space=pltpu.SMEM),
            whole((rows, count)),
            whole((rows, count)),
            whole((all_blocks * slots, 2 * size)),
        ],
        out_shape=[
            jax.ShapeDtypeStruct((rows, count * size), BF16),
            jax.ShapeDtypeStruct((rows, count * size), F32),
        ],
        scratch_shapes=[
            pltpu.VMEM((all_blocks * slots, 2 * size), F32),
            pltpu.VMEM((16, count * size), F32),
            pltpu.VMEM((16, count * size), F32),
        ],
        compiler_params=params(),
    )(place.T.reshape(-1), scale.T, mass.T, returned.reshape(all_blocks * slots, 2 * size))

    new_centroids = sums.reshape(blocks * size, depth).astype(F32)
    return soft_codes, candidate_scores, new_centroids, cluster_mass.reshape(blocks * size)


def solution(mesh):
    rows = P(("dp", "clus"), None)
    return jax.shard_map(
        body,
        mesh=mesh,
        in_specs=(rows, rows, rows, P("clus"), P("clus", None), P("clus", None)),
        out_specs=(rows, rows, P("clus", None), P("clus")),
        check_vma=False,
    )
```

```python
import functools

import jax
import jax.numpy as jnp
from jax import lax
from jax.experimental import pallas as pl
from jax.experimental.pallas import tpu as pltpu
from jax.sharding import PartitionSpec as P

F32, BF16, I32 = jnp.float32, jnp.bfloat16, jnp.int32
MESH = pl.DeviceIdType.MESH
VMEM_LIMIT = 62 << 20

ORDER = (
    (0, 0), (1, 0), (3, 0), (0, 1), (0, 3), (1, 1), (1, 3), (3, 1),
    (3, 3), (2, 0), (0, 2), (2, 1), (1, 2), (2, 3), (3, 2), (2, 2),
)
WAVES = (0, 12, 24, 32)
CUTS = (14, 18, 22, 26)
RING = (0, 1, 3, 2)


def packed_table(values):
    word = sum(v << (2 * i) for i, v in enumerate(values))
    return word - (1 << 32) if word >= 1 << 31 else word


TABLE_Y = packed_table([o[0] for o in ORDER])
TABLE_Z = packed_table([o[1] for o in ORDER])


def entry(table, index):
    return lax.shift_right_logical(jnp.int32(table), jnp.int32(2) * index) % 4


def strict_upper(size):
    row = lax.broadcasted_iota(I32, (size, size), 0)
    column = lax.broadcasted_iota(I32, (size, size), 1)
    return jnp.where(row < column, 1.0, 0.0).astype(BF16)


def three(x):
    high = x.astype(BF16)
    rest = x - high.astype(F32)
    middle = rest.astype(BF16)
    low = (rest - middle.astype(F32)).astype(BF16)
    return high, middle, low


def prepare_kernel(all_blocks, slots, packed_ref, rows_ref, ext_ref, slot_ref):
    parents, rows = packed_ref.shape
    depth = rows_ref.shape[1]
    named = lax.shift_right_logical(packed_ref[...], 1)
    kind = packed_ref[...] & 1
    ids = jnp.concatenate([named.astype(F32), kind.astype(F32)], axis=0).astype(BF16)
    ext_ref[0:2 * parents, 0:rows] = ids
    ext_ref[0:2 * parents, rows:depth] = jnp.zeros((2 * parents, depth - rows), BF16)
    ext_ref[2 * parents:2 * parents + rows, :] = rows_ref[...]
    number = lax.broadcasted_iota(I32, (all_blocks, rows), 0)
    hit = jnp.zeros((all_blocks, rows), F32)
    for j in range(parents):
        hit = hit + jnp.where(named[j:j + 1] == number, 1.0, 0.0)
    rank = jnp.dot(hit.astype(BF16), strict_upper(rows), preferred_element_type=F32)
    for j in range(parents):
        own = jnp.sum(jnp.where(named[j:j + 1] == number, rank, 0.0), axis=0, keepdims=True)
        slot_ref[j:j + 1, :] = named[j:j + 1] * slots + own.astype(I32)


def fused_kernel(
    temper_ref, slot_ref, ext_ref, place_ref, two_ref, three_ref,
    buf_ref, fin_ref, total_ref, codes_ref, deeper_ref,
    rowbuf, w2, w3, g, et, pay, child, upper, stats, stat_out, stat_in, onehot, item_rank, back_out, back_in,
    sc, part, relay_in, near_in, own, mass_all, mass_send, column_scr,
    ret_ref, wide, scale_mass, code_rows, deep_rows, out_sem,
    load_sem, w_sem, local_sem, ring_send, ring_recv, sib_send, sib_recv, pay_send, pay_recv,
    stat_send, stat_recv, back_send, back_recv, dp_send, dp_recv,
):
    parents, rows = place_ref.shape
    total_rows, depth = ext_ref.shape
    slots = 32
    blocks = temper_ref.shape[0]
    size = w2.shape[0] // blocks
    shards = buf_ref.shape[0]
    all_blocks = blocks * shards
    dp = lax.axis_index("dp")
    me = lax.axis_index("clus")
    core = me % 2
    z = (me // 2) % 4
    y = me // 8
    sibling = me + 1 - 2 * core

    def at(dy, dz, flip=0):
        return (((y + dy) % 4) * 4 + (z + dz) % 4) * 2 + (core + flip) % 2

    def source(p):
        q = p // 2
        return at(entry(TABLE_Y, q), entry(TABLE_Z, q), p % 2)

    def holder(p):
        q = p // 2
        return at(4 - entry(TABLE_Y, q), 4 - entry(TABLE_Z, q), p % 2)

    barrier = pltpu.get_barrier_semaphore()

    @pl.loop(1, shards)
    def _(d):
        pl.semaphore_signal(barrier, inc=1, device_id=(dp, (me + d) % shards), device_id_type=MESH)

    for d in (1, 2, 3):
        pl.semaphore_signal(barrier, inc=1, device_id=((dp + d) % 4, me), device_id_type=MESH)
    pl.semaphore_wait(barrier, shards - 1 + 3)

    quarter = rows // 4
    ids = total_rows - rows
    piece = {
        "A": (0, ids + 2 * quarter), "A0": (0, ids + quarter), "A1": (ids + quarter, quarter),
        "B": (ids + 2 * quarter, 2 * quarter), "B0": (ids + 2 * quarter, quarter), "B1": (ids + 3 * quarter, quarter),
    }

    def part_of(ref, name):
        start, length = piece[name]
        return ref.at[pl.ds(start, length), :]

    def chip(half, first, second):
        return (first, second) if half == "A" else (second, first)

    def ring(half, k, offset, name, step):
        index = (0 if half == "A" else 20) + k
        block = at(*offset)
        mine = ext_ref if offset == (0, 0) else buf_ref.at[block]
        return pltpu.make_async_remote_copy(
            src_ref=part_of(mine, name), dst_ref=part_of(buf_ref.at[block], name),
            send_sem=ring_send.at[index], recv_sem=ring_recv.at[index],
            device_id=(dp, at(*step)), device_id_type=MESH,
        )

    def arrival(half, k, offset, name):
        index = (0 if half == "A" else 20) + k
        block = at(*offset)
        return pltpu.make_async_remote_copy(
            src_ref=part_of(buf_ref.at[block], name), dst_ref=part_of(buf_ref.at[block], name),
            send_sem=ring_send.at[index], recv_sem=ring_recv.at[index],
            device_id=(dp, at(1, 0)), device_id_type=MESH,
        )

    sent = []

    def go(copy):
        copy.start()
        sent.append(copy)

    def share(half, offset):
        index = (0 if half == "A" else 16) + ORDER.index(offset)
        block = at(*offset)
        mine = ext_ref if offset == (0, 0) else buf_ref.at[block]
        go(pltpu.make_async_remote_copy(
            src_ref=part_of(mine, half), dst_ref=part_of(buf_ref.at[block], half),
            send_sem=sib_send.at[index], recv_sem=sib_recv.at[index],
            device_id=(dp, sibling), device_id_type=MESH,
        ))

    def shared(half, q):
        index = (0 if half == "A" else 16) + q
        block = at(*ORDER[q], 1)
        pltpu.make_async_remote_copy(
            src_ref=part_of(buf_ref.at[block], half), dst_ref=part_of(buf_ref.at[block], half),
            send_sem=sib_send.at[index], recv_sem=sib_recv.at[index],
            device_id=(dp, sibling), device_id_type=MESH,
        ).wait_recv()

    def first_axis(half, step):
        return chip(half, step, 0)

    def second_axis(half, step):
        return chip(half, 0, step)

    def enter_second(half, i):
        block = chip(half, RING[i], 0)
        go(ring(half, 4 + 4 * i, block, half, second_axis(half, 1)))
        go(ring(half, 5 + 4 * i, block, half, second_axis(half, 3)))

    def first_near(half):
        arrival(half, 1, chip(half, 1, 0), half).wait_recv()
        go(ring(half, 3, chip(half, 1, 0), half + "1", first_axis(half, 3)))
        arrival(half, 0, chip(half, 3, 0), half).wait_recv()
        go(ring(half, 2, chip(half, 3, 0), half + "0", first_axis(half, 1)))

    def first_near_on(half):
        enter_second(half, 1)
        enter_second(half, 2)
        share(half, chip(half, 1, 0))
        share(half, chip(half, 3, 0))

    def first_far(half):
        arrival(half, 2, chip(half, 2, 0), half + "0").wait_recv()
        arrival(half, 3, chip(half, 2, 0), half + "1").wait_recv()
        enter_second(half, 3)
        share(half, chip(half, 2, 0))

    def second_near(half, i):
        o = RING[i]
        arrival(half, 5 + 4 * i, chip(half, o, 1), half).wait_recv()
        go(ring(half, 7 + 4 * i, chip(half, o, 1), half + "1", second_axis(half, 3)))
        arrival(half, 4 + 4 * i, chip(half, o, 3), half).wait_recv()
        go(ring(half, 6 + 4 * i, chip(half, o, 3), half + "0", second_axis(half, 1)))
        share(half, chip(half, o, 1))
        share(half, chip(half, o, 3))

    def second_far(half, i):
        o = RING[i]
        arrival(half, 6 + 4 * i, chip(half, o, 2), half + "0").wait_recv()
        arrival(half, 7 + 4 * i, chip(half, o, 2), half + "1").wait_recv()
        share(half, chip(half, o, 2))

    def load(p):
        return pltpu.make_async_copy(buf_ref.at[source(p)], rowbuf.at[p % 4], load_sem.at[p % 4])

    first_block = (me * blocks).astype(F32)

    def pay_copy(p, index, device):
        return pltpu.make_async_remote_copy(
            src_ref=pay.at[p], dst_ref=ret_ref.at[index], send_sem=pay_send.at[p], recv_sem=pay_recv.at[p],
            device_id=(dp, device), device_id_type=MESH,
        )

    def start_pay(p):
        pay_copy(p, me, source(p)).start()

    def gather(low, high, send=None):
        for q in range(low // 2, high // 2):
            shared("A", q)
            shared("B", q)
        for p in range(low, min(low + 3, high)):
            load(jnp.int32(p)).start()
        slot_id = lax.broadcasted_iota(I32, (slots, rows), 0).astype(F32)
        lane = lax.broadcasted_iota(I32, (slots, 128), 1)

        @pl.loop(low, high)
        def _(p):
            load(p).wait()
            if send is not None:
                start_pay(p + (send - low))

            @pl.when(p + 3 < high)
            def _():
                load(p + 3).start()

            meta = rowbuf[p % 4, 0:2 * parents, 0:rows].astype(F32)
            block = meta[:parents] - first_block
            kind = meta[parents:]
            hits, kinds = [], []
            for b in range(blocks):
                match = block == float(b)
                hits.append(jnp.sum(jnp.where(match, 1.0, 0.0), axis=0, keepdims=True))
                kinds.append(jnp.sum(jnp.where(match, kind, 0.0), axis=0, keepdims=True))
            hit = jnp.concatenate(hits, axis=0)
            rank = jnp.dot(hit.astype(BF16), upper[...], preferred_element_type=F32)
            rank = jnp.where(hit > 0.0, rank, -1.0)
            selects = []
            child_lanes = jnp.zeros((slots, 128), F32)
            for b in range(blocks):
                select = slot_id == rank[b:b + 1]
                column = jnp.sum(jnp.where(select, kinds[b], 0.0), axis=1, keepdims=True)
                child_lanes = jnp.where(lane == b, column, child_lanes)
                selects.append(jnp.where(select, 1.0, 0.0).astype(BF16))
            select = jnp.concatenate(selects, axis=0)
            picked = jnp.dot(
                select, rowbuf[p % 4, ids:total_rows, :], preferred_element_type=F32
            ).astype(BF16)
            place = pl.ds(pl.multiple_of(p * slots, slots), slots)
            child[place, :] = child_lanes
            for b in range(blocks):
                g[b, place, :] = picked[b * slots:(b + 1) * slots]

    contract_last = (((1,), (1,)), ((), ()))

    def score(wave, low, high, send=None):
        start, count = WAVES[wave] * slots, (WAVES[wave + 1] - WAVES[wave]) * slots
        here = slice(start, start + count)
        lane = lax.broadcasted_iota(I32, (count, 128), 1)

        @pl.loop(low, high)
        def _(b):
            if send is not None:
                @pl.when(b % 2 == 0)
                def _():
                    start_pay(b // 2 + send)

            x = g[b, here, :]
            near = lax.dot_general(
                x, w2[pl.ds(pl.multiple_of(b * size, size), size), :], contract_last, preferred_element_type=F32
            )
            far = lax.dot_general(
                x, w3[pl.ds(pl.multiple_of(b * 2 * size, 2 * size), 2 * size), :], contract_last,
                preferred_element_type=F32,
            )
            value = near * temper_ref[b]
            which = jnp.sum(jnp.where(lane == b, child[here, :], 0.0), axis=1, keepdims=True)
            deeper = jnp.where(which > 0.5, far[:, size:], far[:, :size]).astype(BF16)
            most = jnp.max(value, axis=1, keepdims=True)
            weight = jnp.exp(value - most)
            amount = jnp.sum(weight, axis=1, keepdims=True)
            old = stats[here, :]
            stats[here, :] = jnp.where(lane == b, most, jnp.where(lane == b + blocks, amount, old))
            et[b, :, here] = weight.T
            weight = weight.astype(BF16)
            place = pl.ds(pl.multiple_of(b * slots, slots), slots)
            for i in range(count // slots):
                pay[WAVES[wave] + i, place, 0:size] = weight[i * slots:(i + 1) * slots]
                pay[WAVES[wave] + i, place, size:2 * size] = deeper[i * slots:(i + 1) * slots]

    def each(low, high, action):
        @pl.loop(max(low, 1), high)
        def _(p):
            action(p)

    def stat_copy(p, index, device):
        return pltpu.make_async_remote_copy(
            src_ref=stat_out.at[p], dst_ref=stat_in.at[index], send_sem=stat_send.at[p], recv_sem=stat_recv.at[p],
            device_id=(dp, device), device_id_type=MESH,
        )

    def send_stats(wave):
        low, high = WAVES[wave], WAVES[wave + 1]
        for t in range(low // 4, high // 4):
            flipped = stats[t * 128:(t + 1) * 128, :].T[0:2 * blocks, :]
            for s in range(4):
                moved = flipped if s == 0 else pltpu.roll(flipped, 128 - s * slots, 1)
                stat_out[t * 4 + s] = moved
        if low == 0:
            stat_in[me] = stat_out[0]
        each(low, high, lambda p: stat_copy(p, me, source(p)).start())

    def send_pay(low, high):
        each(low, high, start_pay)

    def back_copy(p, index, device):
        return pltpu.make_async_remote_copy(
            src_ref=back_out.at[index], dst_ref=back_in.at[p], send_sem=back_send.at[p], recv_sem=back_recv.at[p],
            device_id=(dp, device), device_id_type=MESH,
        )

    for half, step in (("A", 1), ("B", 1)):
        go(ring(half, 0, (0, 0), half, first_axis(half, 1)))
        go(ring(half, 1, (0, 0), half, first_axis(half, 3)))
    enter_second("A", 0)
    enter_second("B", 0)
    share("A", (0, 0))
    share("B", (0, 0))
    in_two = pltpu.make_async_copy(two_ref, w2, w_sem.at[0])
    in_three = pltpu.make_async_copy(three_ref, w3, w_sem.at[1])
    in_two.start()
    in_three.start()
    own_in = pltpu.make_async_copy(ext_ref, rowbuf.at[0], local_sem.at[0])
    own_in.start()
    upper[...] = strict_upper(rows)
    stats[...] = jnp.zeros_like(stats)
    back_out[...] = jnp.zeros_like(back_out)
    own_in.wait()
    own_out = pltpu.make_async_copy(rowbuf.at[0], buf_ref.at[me], local_sem.at[1])
    own_out.start()

    named = lax.shift_right_logical(place_ref[...], 5)
    item_rank[...] = (place_ref[...] & (slots - 1)).astype(F32)
    number = lax.broadcasted_iota(I32, (all_blocks, rows), 0)
    for j in range(parents):
        onehot[j] = jnp.where(named[j:j + 1] == number, 1.0, 0.0).astype(BF16)
    own_out.wait()

    first_near("A")
    first_near("B")
    first_near_on("A")
    first_near_on("B")
    gather(0, 2)
    second_near("A", 0)
    second_near("B", 0)
    first_far("A")
    first_far("B")
    gather(2, 10)
    second_near("A", 1)
    second_near("B", 1)
    gather(10, 12)
    in_two.wait()
    in_three.wait()
    score(0, 0, blocks)
    second_near("A", 2)
    second_near("B", 2)
    send_stats(0)
    gather(12, 18)
    second_far("A", 0)
    second_far("B", 0)
    gather(18, 22)
    second_near("A", 3)
    second_near("B", 3)
    second_far("A", 1)
    second_far("B", 1)
    gather(22, 26)
    score(1, 0, blocks)
    second_far("A", 2)
    second_far("B", 2)
    second_far("A", 3)
    second_far("B", 3)
    send_stats(1)
    gather(26, 32, 1)
    score(2, 0, blocks, 7)
    send_stats(2)
    send_pay(11, CUTS[0])
    own_pay = pltpu.make_async_copy(pay.at[0], ret_ref.at[me], local_sem.at[0])
    own_pay.start()

    each(0, shards, lambda p: stat_copy(p, holder(p), source(p)).wait_recv())
    table = jnp.concatenate([stat_in[o, 0:blocks, :] for o in range(shards)], axis=0)
    table_sum = jnp.concatenate([stat_in[o, blocks:2 * blocks, :] for o in range(shards)], axis=0)
    both = jnp.concatenate([table.T[0:slots], table_sum.T[0:slots]], axis=0)
    stack = jnp.concatenate(three(both), axis=0)
    slot_row = lax.broadcasted_iota(I32, (slots, rows), 0).astype(F32)
    mosts, amounts = [], []
    for j in range(parents):
        found = jnp.dot(stack, onehot[j], preferred_element_type=F32)
        found = (found[0:2 * slots] + found[2 * slots:4 * slots]) + found[4 * slots:6 * slots]
        pick = slot_row == item_rank[j:j + 1, :]
        mosts.append(jnp.sum(jnp.where(pick, found[0:slots], 0.0), axis=0, keepdims=True))
        amounts.append(jnp.sum(jnp.where(pick, found[slots:], 0.0), axis=0, keepdims=True))
    most = jnp.concatenate(mosts, axis=0)
    amount = jnp.concatenate(amounts, axis=0)
    weight = jnp.exp(most - jnp.max(most, axis=0, keepdims=True))
    scale = weight / jnp.sum(weight * amount, axis=0, keepdims=True)
    blank = jnp.zeros((128 - 2 * parents, rows), F32)
    scale_mass[...] = jnp.concatenate([scale, scale * amount * parents, blank], axis=0).T
    back = jnp.zeros((all_blocks, 4 * slots), F32)
    for j in range(parents):
        pick = slot_row == item_rank[j:j + 1, :]
        spread = jnp.where(pick, scale[j:j + 1, :], 0.0)
        pad = jnp.zeros((slots, rows), BF16)
        stacked = jnp.concatenate(three(spread) + (pad,), axis=0)
        back = back + lax.dot_general(onehot[j], stacked, contract_last, preferred_element_type=F32)
    back = (back + pltpu.roll(back, 3 * slots, 1)) + pltpu.roll(back, 2 * slots, 1)
    for o in range(shards):
        back_out[o] = back[o * blocks:(o + 1) * blocks, :]
    back_in[0] = back_out[me]
    each(0, shards, lambda p: back_copy(p, holder(p), holder(p)).start())
    send_pay(CUTS[0], CUTS[1])
    each(0, shards, lambda p: back_copy(p, holder(p), holder(p)).wait_recv())
    lane8 = lax.broadcasted_iota(I32, (blocks, 128), 1)
    for t in range(shards // 4):
        joined = back_in[4 * t]
        for s in range(1, 4):
            joined = jnp.where(lane8 >= s * slots, pltpu.roll(back_in[4 * t + s], s * slots, 1), joined)
        sc[:, t * 128:(t + 1) * 128] = joined

    def sums(b):
        codes = et[b] * sc[pl.ds(b, 1), :]
        high = codes.astype(BF16)
        low = (codes - high.astype(F32)).astype(BF16)
        product = jnp.dot(jnp.concatenate([high, low], axis=0), g[b], preferred_element_type=F32)
        return product[:size] + product[size:], jnp.sum(codes, axis=1, keepdims=True)

    lane128 = lax.broadcasted_iota(I32, (size, 128), 1)
    column_scr[...] = jnp.zeros_like(column_scr)

    def sum_blocks(first, low, high):
        @pl.loop(low, high)
        def _(i):
            b = (2 * first + i) % blocks
            value, column = sums(b)
            part[b] = value
            column_scr[...] = jnp.where(lane128 == b, column, column_scr[...])

    def widen(low, high):
        @pl.loop(low, high)
        def _(o):
            here = pl.ds(pl.multiple_of(o * blocks * slots, blocks * slots), blocks * slots)
            wide[here, :] = ret_ref[o].astype(F32)

    def spread_rows(low, high):
        @pl.loop(low, high)
        def _(i):
            for r in range(16):
                for j in range(parents):
                    item = wide[pl.ds(slot_ref[j, i * 16 + r], 1), :]
                    code_rows[r:r + 1, j * size:(j + 1) * size] = item[:, :size]
                    deep_rows[r:r + 1, j * size:(j + 1) * size] = item[:, size:]
            here = pl.ds(pl.multiple_of(i * 16, 16), 16)
            low_rows = pl.ds(pl.multiple_of((i % 8) * 16, 16), 16)
            factors = scale_mass[here, :]
            for j in range(parents):
                part_j = slice(j * size, (j + 1) * size)
                g[0, here, part_j] = (code_rows[:, part_j] * factors[:, j:j + 1]).astype(BF16)
                part[i // 8, low_rows, part_j] = deep_rows[:, part_j] * factors[:, parents + j:parents + j + 1]

    def dp_copy(index, source_ref, target_ref, step):
        return pltpu.make_async_remote_copy(
            src_ref=source_ref, dst_ref=target_ref, send_sem=dp_send.at[index], recv_sem=dp_recv.at[index],
            device_id=((dp + step) % 4, me), device_id_type=MESH,
        )

    right, left, across = (dp + 1) % 4, (dp + 3) % 4, (dp + 2) % 4
    sum_blocks(across, 0, 2)
    own[0] = part[2 * across].astype(BF16)
    own[1] = part[2 * across + 1].astype(BF16)
    relay = [dp_copy(0, own.at[0], relay_in.at[0], 1), dp_copy(1, own.at[1], relay_in.at[1], 3)]
    for copy in relay:
        copy.start()
    send_pay(CUTS[1], CUTS[2])
    sum_blocks(across, 2, 4)
    sum_blocks(across, 6, 8)
    own[3] = part[2 * right + 1].astype(BF16)
    own[4] = part[2 * left].astype(BF16)
    near = [
        dp_copy(2, own.at[2], near_in.at[0], 1), dp_copy(3, own.at[3], near_in.at[1], 1),
        dp_copy(4, own.at[4], near_in.at[2], 3), dp_copy(5, own.at[5], near_in.at[3], 3),
    ]
    near[1].start()
    near[2].start()
    send_pay(CUTS[2], CUTS[3])
    sum_blocks(across, 4, 6)
    mass_send[...] = column_scr[...].T[0:blocks, :]
    mass_all[dp] = mass_send[...]
    mass_copies = [dp_copy(8 + d, mass_send, mass_all.at[dp], d) for d in (1, 2, 3)]
    for copy in mass_copies:
        copy.start()
    relay[0].wait_recv()
    own[2] = (part[2 * right] + relay_in[0].astype(F32)).astype(BF16)
    near[0].start()
    relay[1].wait_recv()
    own[5] = (part[2 * left + 1] + relay_in[1].astype(F32)).astype(BF16)
    near[3].start()
    send_pay(CUTS[3], shards)
    for copy in mass_copies:
        copy.wait_recv()
    all_mass = ((mass_all[0] + mass_all[1]) + mass_all[2]) + mass_all[3]
    total_ref[...] = all_mass
    spare = jnp.zeros((128 - blocks, 128), F32)
    column_scr[...] = jnp.maximum(jnp.concatenate([all_mass, spare], axis=0), 1.0).T
    for copy in near:
        copy.wait_recv()
    for i in range(2):
        b = 2 * dp + i
        column = jnp.sum(jnp.where(lane128 == b, column_scr[...], 0.0), axis=1, keepdims=True)
        value = part[b] + (near_in[i].astype(F32) + near_in[2 + i].astype(F32))
        own[6 + i] = (value / column).astype(BF16)
    ready = [
        dp_copy(12, own.at[6], fin_ref.at[2 * dp], 1), dp_copy(13, own.at[7], fin_ref.at[2 * dp + 1], 3),
        dp_copy(14, own.at[7], fin_ref.at[2 * dp + 1], 1), dp_copy(15, own.at[6], fin_ref.at[2 * dp], 3),
    ]
    for copy in ready:
        copy.start()
    own_fin = [pltpu.make_async_copy(own.at[6 + i], fin_ref.at[2 * dp + i], local_sem.at[2 + i]) for i in range(2)]
    for copy in own_fin:
        copy.start()
    each(0, shards, lambda p: pay_copy(p, holder(p), source(p)).wait_recv())
    own_pay.wait()
    widen(0, shards)
    dp_copy(12, own.at[6], fin_ref.at[2 * left], 1).wait_recv()
    onward = [dp_copy(6, fin_ref.at[2 * left], fin_ref.at[2 * left], 1)]
    onward[0].start()
    dp_copy(13, own.at[7], fin_ref.at[2 * right + 1], 3).wait_recv()
    onward.append(dp_copy(7, fin_ref.at[2 * right + 1], fin_ref.at[2 * right + 1], 3))
    onward[1].start()
    steps = rows // 16
    spread_rows(0, steps)
    outs = [pltpu.make_async_copy(g.at[0, pl.ds(0, rows), :], codes_ref, out_sem.at[4])]
    for i in range(rows // size):
        outs.append(pltpu.make_async_copy(part.at[i], deeper_ref.at[pl.ds(i * size, size), :], out_sem.at[i]))
    for copy in outs:
        copy.start()
    dp_copy(14, own.at[7], fin_ref.at[2 * left + 1], 1).wait_recv()
    dp_copy(15, own.at[6], fin_ref.at[2 * right], 3).wait_recv()
    dp_copy(6, own.at[6], fin_ref.at[2 * across], 1).wait_recv()
    dp_copy(7, own.at[7], fin_ref.at[2 * across + 1], 3).wait_recv()

    for copy in sent + mass_copies + relay + near + ready + onward:
        copy.wait_send()
    each(0, shards, lambda p: pay_copy(p, me, source(p)).wait_send())
    each(0, shards, lambda p: stat_copy(p, me, source(p)).wait_send())
    each(0, shards, lambda p: back_copy(p, holder(p), holder(p)).wait_send())
    for copy in own_fin + outs:
        copy.wait()


def params():
    return pltpu.CompilerParams(vmem_limit_bytes=VMEM_LIMIT)


def body(embeddings, parents, children, temper, level_two, level_three):
    rows, depth = embeddings.shape
    count = parents.shape[1]
    blocks = temper.shape[0]
    size = level_two.shape[0] // blocks
    kinds = level_three.shape[0] // (blocks * size)
    shards = lax.axis_size("clus")
    all_blocks = blocks * shards
    slots = 2 * rows * count // all_blocks
    assert kinds == 2 and shards == 32 and slots == 32 and blocks == 8 and lax.axis_size("dp") == 4

    packed = (parents * kinds + children).T
    total_rows = rows + 2 * count
    extended, place = pl.pallas_call(
        functools.partial(prepare_kernel, all_blocks, slots),
        out_shape=[jax.ShapeDtypeStruct((total_rows, depth), BF16), jax.ShapeDtypeStruct((count, rows), I32)],
        compiler_params=params(),
    )(packed, embeddings)
    anywhere = pl.BlockSpec(memory_space=pl.ANY)
    vmem = pl.BlockSpec(memory_space=pltpu.VMEM)
    dma = pltpu.SemaphoreType.DMA

    _, sums, cluster_mass, soft_codes, candidate_scores = pl.pallas_call(
        fused_kernel,
        in_specs=[
            pl.BlockSpec(memory_space=pltpu.SMEM), pl.BlockSpec(memory_space=pltpu.SMEM),
            anywhere, vmem, anywhere, anywhere,
        ],
        out_specs=[anywhere, anywhere, vmem, anywhere, anywhere],
        out_shape=[
            jax.ShapeDtypeStruct((shards, total_rows, depth), BF16),
            jax.ShapeDtypeStruct((blocks, size, depth), BF16),
            jax.ShapeDtypeStruct((blocks, size), F32),
            jax.ShapeDtypeStruct((rows, count * size), BF16),
            jax.ShapeDtypeStruct((rows, count * size), F32),
        ],
        scratch_shapes=[
            pltpu.VMEM((4, total_rows, depth), BF16),
            pltpu.VMEM(level_two.shape, BF16),
            pltpu.VMEM(level_three.shape, BF16),
            pltpu.VMEM((blocks, shards * slots, depth), BF16),
            pltpu.VMEM((blocks, size, shards * slots), F32),
            pltpu.VMEM((shards, blocks * slots, 2 * size), BF16),
            pltpu.VMEM((shards * slots, 128), F32),
            pltpu.VMEM((rows, rows), BF16),
            pltpu.VMEM((shards * slots, 128), F32),
            pltpu.VMEM((shards, 2 * blocks, 128), F32),
            pltpu.VMEM((shards, 2 * blocks, 128), F32),
            pltpu.VMEM((count, all_blocks, rows), BF16),
            pltpu.VMEM((count, rows), F32),
            pltpu.VMEM((shards, blocks, 128), F32),
            pltpu.VMEM((shards, blocks, 128), F32),
            pltpu.VMEM((blocks, shards * slots), F32),
            pltpu.VMEM((blocks, size, depth), F32),
            pltpu.VMEM((2, size, depth), BF16),
            pltpu.VMEM((4, size, depth), BF16),
            pltpu.VMEM((8, size, depth), BF16),
            pltpu.VMEM((4, blocks, 128), F32),
            pltpu.VMEM((blocks, 128), F32),
            pltpu.VMEM((size, 128), F32),
            pltpu.VMEM((shards, blocks * slots, 2 * size), BF16),
            pltpu.VMEM((shards * blocks * slots, 2 * size), F32),
            pltpu.VMEM((rows, 128), F32),
            pltpu.VMEM((16, count * size), F32),
            pltpu.VMEM((16, count * size), F32),
            dma((5,)),
            dma((4,)), dma((2,)), dma((4,)), dma((40,)), dma((40,)), dma((32,)), dma((32,)),
            dma((shards,)), dma((shards,)), dma((shards,)), dma((shards,)), dma((shards,)), dma((shards,)),
            dma((16,)), dma((16,)),
        ],
        compiler_params=pltpu.CompilerParams(
            vmem_limit_bytes=VMEM_LIMIT, collective_id=0, has_side_effects=True
        ),
    )(temper, place, extended, place, level_two, level_three)

    new_centroids = sums.reshape(blocks * size, depth).astype(F32)
    return soft_codes, candidate_scores, new_centroids, cluster_mass.reshape(blocks * size)


def solution(mesh):
    rows = P(("dp", "clus"), None)
    return jax.shard_map(
        body,
        mesh=mesh,
        in_specs=(rows, rows, rows, P("clus"), P("clus", None), P("clus", None)),
        out_specs=(rows, rows, P("clus", None), P("clus")),
        check_vma=False,
    )
```

```python
import functools

import jax
import jax.numpy as jnp
from jax import lax
from jax.experimental import pallas as pl
from jax.experimental.pallas import tpu as pltpu
from jax.sharding import PartitionSpec as P

F32, BF16, I32 = jnp.float32, jnp.bfloat16, jnp.int32
MESH = pl.DeviceIdType.MESH
VMEM_LIMIT = 62 << 20

ORDER = (
    (0, 0), (1, 0), (0, 1), (3, 0), (0, 3), (1, 1), (1, 3), (3, 1),
    (3, 3), (2, 0), (0, 2), (2, 1), (1, 2), (2, 3), (3, 2), (2, 2),
)
WAVES = (0, 12, 24, 32)
CUTS = (14, 18, 22, 26)
RING = (0, 1, 3, 2)


def packed_table(values):
    word = sum(v << (2 * i) for i, v in enumerate(values))
    return word - (1 << 32) if word >= 1 << 31 else word


TABLE_Y = packed_table([o[0] for o in ORDER])
TABLE_Z = packed_table([o[1] for o in ORDER])


def entry(table, index):
    return lax.shift_right_logical(jnp.int32(table), jnp.int32(2) * index) % 4


def strict_upper(size):
    row = lax.broadcasted_iota(I32, (size, size), 0)
    column = lax.broadcasted_iota(I32, (size, size), 1)
    return jnp.where(row < column, 1.0, 0.0).astype(BF16)


def three(x):
    high = x.astype(BF16)
    rest = x - high.astype(F32)
    middle = rest.astype(BF16)
    low = (rest - middle.astype(F32)).astype(BF16)
    return high, middle, low


def prepare_kernel(all_blocks, slots, packed_ref, rows_ref, ext_ref, slot_ref):
    parents, rows = packed_ref.shape
    depth = rows_ref.shape[1]
    named = lax.shift_right_logical(packed_ref[...], 1)
    kind = packed_ref[...] & 1
    ids = jnp.concatenate([named.astype(F32), kind.astype(F32)], axis=0).astype(BF16)
    ext_ref[0:2 * parents, 0:rows] = ids
    ext_ref[0:2 * parents, rows:depth] = jnp.zeros((2 * parents, depth - rows), BF16)
    ext_ref[2 * parents:2 * parents + rows, :] = rows_ref[...]
    number = lax.broadcasted_iota(I32, (all_blocks, rows), 0)
    hit = jnp.zeros((all_blocks, rows), F32)
    for j in range(parents):
        hit = hit + jnp.where(named[j:j + 1] == number, 1.0, 0.0)
    rank = jnp.dot(hit.astype(BF16), strict_upper(rows), preferred_element_type=F32)
    for j in range(parents):
        own = jnp.sum(jnp.where(named[j:j + 1] == number, rank, 0.0), axis=0, keepdims=True)
        slot_ref[j:j + 1, :] = named[j:j + 1] * slots + own.astype(I32)


def fused_kernel(
    temper_ref, slot_ref, ext_ref, place_ref, two_ref, three_ref,
    buf_ref, fin_ref, total_ref, codes_ref, deeper_ref,
    rowbuf, w2, w3, g, et, pay, child, upper, stats, stat_out, stat_in, onehot, item_rank, back_out, back_in,
    sc, part, relay_in, near_in, own, mass_all, mass_send, column_scr,
    ret_ref, wide, scale_mass, code_rows, deep_rows, out_sem,
    load_sem, w_sem, local_sem, ring_send, ring_recv, sib_send, sib_recv, pay_send, pay_recv,
    stat_send, stat_recv, back_send, back_recv, dp_send, dp_recv,
):
    parents, rows = place_ref.shape
    total_rows, depth = ext_ref.shape
    slots = 32
    blocks = temper_ref.shape[0]
    size = w2.shape[0] // blocks
    shards = buf_ref.shape[0]
    all_blocks = blocks * shards
    dp = lax.axis_index("dp")
    me = lax.axis_index("clus")
    core = me % 2
    z = (me // 2) % 4
    y = me // 8
    sibling = me + 1 - 2 * core

    def at(dy, dz, flip=0):
        return (((y + dy) % 4) * 4 + (z + dz) % 4) * 2 + (core + flip) % 2

    def source(p):
        q = p // 2
        return at(entry(TABLE_Y, q), entry(TABLE_Z, q), p % 2)

    def holder(p):
        q = p // 2
        return at(4 - entry(TABLE_Y, q), 4 - entry(TABLE_Z, q), p % 2)

    barrier = pltpu.get_barrier_semaphore()

    @pl.loop(1, shards)
    def _(d):
        pl.semaphore_signal(barrier, inc=1, device_id=(dp, (me + d) % shards), device_id_type=MESH)

    for d in (1, 2, 3):
        pl.semaphore_signal(barrier, inc=1, device_id=((dp + d) % 4, me), device_id_type=MESH)
    pl.semaphore_wait(barrier, shards - 1 + 3)

    quarter = rows // 4
    ids = total_rows - rows
    piece = {
        "A": (0, ids + 2 * quarter), "A0": (0, ids + quarter), "A1": (ids + quarter, quarter),
        "B": (ids + 2 * quarter, 2 * quarter), "B0": (ids + 2 * quarter, quarter), "B1": (ids + 3 * quarter, quarter),
    }

    def part_of(ref, name):
        start, length = piece[name]
        return ref.at[pl.ds(start, length), :]

    def chip(half, first, second):
        return (first, second) if half == "A" else (second, first)

    def ring(half, k, offset, name, step):
        index = (0 if half == "A" else 20) + k
        block = at(*offset)
        mine = ext_ref if offset == (0, 0) else buf_ref.at[block]
        return pltpu.make_async_remote_copy(
            src_ref=part_of(mine, name), dst_ref=part_of(buf_ref.at[block], name),
            send_sem=ring_send.at[index], recv_sem=ring_recv.at[index],
            device_id=(dp, at(*step)), device_id_type=MESH,
        )

    def arrival(half, k, offset, name):
        index = (0 if half == "A" else 20) + k
        block = at(*offset)
        return pltpu.make_async_remote_copy(
            src_ref=part_of(buf_ref.at[block], name), dst_ref=part_of(buf_ref.at[block], name),
            send_sem=ring_send.at[index], recv_sem=ring_recv.at[index],
            device_id=(dp, at(1, 0)), device_id_type=MESH,
        )

    sent = []

    def go(copy):
        copy.start()
        sent.append(copy)

    def share(half, offset):
        index = (0 if half == "A" else 16) + ORDER.index(offset)
        block = at(*offset)
        mine = ext_ref if offset == (0, 0) else buf_ref.at[block]
        go(pltpu.make_async_remote_copy(
            src_ref=part_of(mine, half), dst_ref=part_of(buf_ref.at[block], half),
            send_sem=sib_send.at[index], recv_sem=sib_recv.at[index],
            device_id=(dp, sibling), device_id_type=MESH,
        ))

    def shared(half, q):
        index = (0 if half == "A" else 16) + q
        block = at(*ORDER[q], 1)
        pltpu.make_async_remote_copy(
            src_ref=part_of(buf_ref.at[block], half), dst_ref=part_of(buf_ref.at[block], half),
            send_sem=sib_send.at[index], recv_sem=sib_recv.at[index],
            device_id=(dp, sibling), device_id_type=MESH,
        ).wait_recv()

    def first_axis(half, step):
        return chip(half, step, 0)

    def second_axis(half, step):
        return chip(half, 0, step)

    def enter_second(half, i):
        block = chip(half, RING[i], 0)
        go(ring(half, 4 + 4 * i, block, half, second_axis(half, 1)))
        go(ring(half, 5 + 4 * i, block, half, second_axis(half, 3)))

    def first_near(half):
        arrival(half, 1, chip(half, 1, 0), half).wait_recv()
        go(ring(half, 3, chip(half, 1, 0), half + "1", first_axis(half, 3)))
        arrival(half, 0, chip(half, 3, 0), half).wait_recv()
        go(ring(half, 2, chip(half, 3, 0), half + "0", first_axis(half, 1)))

    def first_near_on(half):
        enter_second(half, 1)
        enter_second(half, 2)
        share(half, chip(half, 1, 0))
        share(half, chip(half, 3, 0))

    def first_far(half):
        arrival(half, 2, chip(half, 2, 0), half + "0").wait_recv()
        arrival(half, 3, chip(half, 2, 0), half + "1").wait_recv()
        enter_second(half, 3)
        share(half, chip(half, 2, 0))

    def second_near(half, i):
        o = RING[i]
        arrival(half, 5 + 4 * i, chip(half, o, 1), half).wait_recv()
        go(ring(half, 7 + 4 * i, chip(half, o, 1), half + "1", second_axis(half, 3)))
        arrival(half, 4 + 4 * i, chip(half, o, 3), half).wait_recv()
        go(ring(half, 6 + 4 * i, chip(half, o, 3), half + "0", second_axis(half, 1)))
        share(half, chip(half, o, 1))
        share(half, chip(half, o, 3))

    def second_far(half, i):
        o = RING[i]
        arrival(half, 6 + 4 * i, chip(half, o, 2), half + "0").wait_recv()
        arrival(half, 7 + 4 * i, chip(half, o, 2), half + "1").wait_recv()
        share(half, chip(half, o, 2))

    def load(p):
        return pltpu.make_async_copy(buf_ref.at[source(p)], rowbuf.at[p % 4], load_sem.at[p % 4])

    first_block = (me * blocks).astype(F32)

    def pay_copy(p, index, device):
        return pltpu.make_async_remote_copy(
            src_ref=pay.at[p], dst_ref=ret_ref.at[index], send_sem=pay_send.at[p], recv_sem=pay_recv.at[p],
            device_id=(dp, device), device_id_type=MESH,
        )

    def start_pay(k):
        p = (k // 8) * 8 + (k % 4) * 2 + (k % 8) // 4
        pay_copy(p, me, source(p)).start()

    def gather(low, high, send=None):
        for q in range(low // 2, high // 2):
            shared("A", q)
            shared("B", q)
        for p in range(low, min(low + 3, high)):
            load(jnp.int32(p)).start()
        slot_id = lax.broadcasted_iota(I32, (slots, rows), 0).astype(F32)
        lane = lax.broadcasted_iota(I32, (slots, 128), 1)

        @pl.loop(low, high)
        def _(p):
            load(p).wait()
            if send is not None:
                start_pay(p + (send - low))

            @pl.when(p + 3 < high)
            def _():
                load(p + 3).start()

            meta = rowbuf[p % 4, 0:2 * parents, 0:rows].astype(F32)
            block = meta[:parents] - first_block
            kind = meta[parents:]
            hits, kinds = [], []
            for b in range(blocks):
                match = block == float(b)
                hits.append(jnp.sum(jnp.where(match, 1.0, 0.0), axis=0, keepdims=True))
                kinds.append(jnp.sum(jnp.where(match, kind, 0.0), axis=0, keepdims=True))
            hit = jnp.concatenate(hits, axis=0)
            rank = jnp.dot(hit.astype(BF16), upper[...], preferred_element_type=F32)
            rank = jnp.where(hit > 0.0, rank, -1.0)
            selects = []
            child_lanes = jnp.zeros((slots, 128), F32)
            for b in range(blocks):
                select = slot_id == rank[b:b + 1]
                column = jnp.sum(jnp.where(select, kinds[b], 0.0), axis=1, keepdims=True)
                child_lanes = jnp.where(lane == b, column, child_lanes)
                selects.append(jnp.where(select, 1.0, 0.0).astype(BF16))
            select = jnp.concatenate(selects, axis=0)
            picked = jnp.dot(
                select, rowbuf[p % 4, ids:total_rows, :], preferred_element_type=F32
            ).astype(BF16)
            place = pl.ds(pl.multiple_of(p * slots, slots), slots)
            child[place, :] = child_lanes
            for b in range(blocks):
                g[b, place, :] = picked[b * slots:(b + 1) * slots]

    contract_last = (((1,), (1,)), ((), ()))

    def score(wave, low, high, send=None):
        start, count = WAVES[wave] * slots, (WAVES[wave + 1] - WAVES[wave]) * slots
        here = slice(start, start + count)
        lane = lax.broadcasted_iota(I32, (count, 128), 1)

        @pl.loop(low, high)
        def _(b):
            if send is not None:
                @pl.when(b % 2 == 0)
                def _():
                    start_pay(b // 2 + send)

            x = g[b, here, :]
            near = lax.dot_general(
                x, w2[pl.ds(pl.multiple_of(b * size, size), size), :], contract_last, preferred_element_type=F32
            )
            far = lax.dot_general(
                x, w3[pl.ds(pl.multiple_of(b * 2 * size, 2 * size), 2 * size), :], contract_last,
                preferred_element_type=F32,
            )
            value = near * temper_ref[b]
            which = jnp.sum(jnp.where(lane == b, child[here, :], 0.0), axis=1, keepdims=True)
            deeper = jnp.where(which > 0.5, far[:, size:], far[:, :size]).astype(BF16)
            most = jnp.max(value, axis=1, keepdims=True)
            weight = jnp.exp(value - most)
            amount = jnp.sum(weight, axis=1, keepdims=True)
            old = stats[here, :]
            stats[here, :] = jnp.where(lane == b, most, jnp.where(lane == b + blocks, amount, old))
            et[b, :, here] = weight.T
            weight = weight.astype(BF16)
            place = pl.ds(pl.multiple_of(b * slots, slots), slots)
            for i in range(count // slots):
                pay[WAVES[wave] + i, place, 0:size] = weight[i * slots:(i + 1) * slots]
                pay[WAVES[wave] + i, place, size:2 * size] = deeper[i * slots:(i + 1) * slots]

    def each(low, high, action):
        @pl.loop(max(low, 1), high)
        def _(p):
            action(p)

    def stat_copy(p, index, device):
        return pltpu.make_async_remote_copy(
            src_ref=stat_out.at[p], dst_ref=stat_in.at[index], send_sem=stat_send.at[p], recv_sem=stat_recv.at[p],
            device_id=(dp, device), device_id_type=MESH,
        )

    def send_stats(wave):
        low, high = WAVES[wave], WAVES[wave + 1]
        for t in range(low // 4, high // 4):
            flipped = stats[t * 128:(t + 1) * 128, :].T[0:2 * blocks, :]
            for s in range(4):
                moved = flipped if s == 0 else pltpu.roll(flipped, 128 - s * slots, 1)
                stat_out[t * 4 + s] = moved
        if low == 0:
            stat_in[me] = stat_out[0]
        each(low, high, lambda p: stat_copy(p, me, source(p)).start())

    def send_pay(low, high):
        each(low, high, start_pay)

    def back_copy(p, index, device):
        return pltpu.make_async_remote_copy(
            src_ref=back_out.at[index], dst_ref=back_in.at[p], send_sem=back_send.at[p], recv_sem=back_recv.at[p],
            device_id=(dp, device), device_id_type=MESH,
        )

    for half, step in (("A", 1), ("B", 1)):
        go(ring(half, 0, (0, 0), half, first_axis(half, 1)))
        go(ring(half, 1, (0, 0), half, first_axis(half, 3)))
    enter_second("A", 0)
    enter_second("B", 0)
    share("A", (0, 0))
    share("B", (0, 0))
    in_two = pltpu.make_async_copy(two_ref, w2, w_sem.at[0])
    in_three = pltpu.make_async_copy(three_ref, w3, w_sem.at[1])
    in_two.start()
    in_three.start()
    own_in = pltpu.make_async_copy(ext_ref, rowbuf.at[0], local_sem.at[0])
    own_in.start()
    upper[...] = strict_upper(rows)
    stats[...] = jnp.zeros_like(stats)
    back_out[...] = jnp.zeros_like(back_out)
    own_in.wait()
    own_out = pltpu.make_async_copy(rowbuf.at[0], buf_ref.at[me], local_sem.at[1])
    own_out.start()

    named = lax.shift_right_logical(place_ref[...], 5)
    item_rank[...] = (place_ref[...] & (slots - 1)).astype(F32)
    number = lax.broadcasted_iota(I32, (all_blocks, rows), 0)
    for j in range(parents):
        onehot[j] = jnp.where(named[j:j + 1] == number, 1.0, 0.0).astype(BF16)
    own_out.wait()

    first_near("A")
    first_near("B")
    first_near_on("A")
    first_near_on("B")
    gather(0, 2)
    second_near("A", 0)
    second_near("B", 0)
    first_far("A")
    first_far("B")
    gather(2, 10)
    second_near("A", 1)
    second_near("B", 1)
    gather(10, 12)
    in_two.wait()
    in_three.wait()
    score(0, 0, blocks)
    second_near("A", 2)
    second_near("B", 2)
    send_stats(0)
    gather(12, 18)
    second_far("A", 0)
    second_far("B", 0)
    gather(18, 22)
    second_near("A", 3)
    second_near("B", 3)
    second_far("A", 1)
    second_far("B", 1)
    gather(22, 26)
    score(1, 0, blocks)
    second_far("A", 2)
    second_far("B", 2)
    second_far("A", 3)
    second_far("B", 3)
    send_stats(1)
    gather(26, 32, 1)
    score(2, 0, blocks, 7)
    send_stats(2)
    send_pay(11, CUTS[0])
    own_pay = pltpu.make_async_copy(pay.at[0], ret_ref.at[me], local_sem.at[0])
    own_pay.start()

    each(0, shards, lambda p: stat_copy(p, holder(p), source(p)).wait_recv())
    table = jnp.concatenate([stat_in[o, 0:blocks, :] for o in range(shards)], axis=0)
    table_sum = jnp.concatenate([stat_in[o, blocks:2 * blocks, :] for o in range(shards)], axis=0)
    both = jnp.concatenate([table.T[0:slots], table_sum.T[0:slots]], axis=0)
    stack = jnp.concatenate(three(both), axis=0)
    slot_row = lax.broadcasted_iota(I32, (slots, rows), 0).astype(F32)
    mosts, amounts = [], []
    for j in range(parents):
        found = jnp.dot(stack, onehot[j], preferred_element_type=F32)
        found = (found[0:2 * slots] + found[2 * slots:4 * slots]) + found[4 * slots:6 * slots]
        pick = slot_row == item_rank[j:j + 1, :]
        mosts.append(jnp.sum(jnp.where(pick, found[0:slots], 0.0), axis=0, keepdims=True))
        amounts.append(jnp.sum(jnp.where(pick, found[slots:], 0.0), axis=0, keepdims=True))
    most = jnp.concatenate(mosts, axis=0)
    amount = jnp.concatenate(amounts, axis=0)
    weight = jnp.exp(most - jnp.max(most, axis=0, keepdims=True))
    scale = weight / jnp.sum(weight * amount, axis=0, keepdims=True)
    blank = jnp.zeros((128 - 2 * parents, rows), F32)
    scale_mass[...] = jnp.concatenate([scale, scale * amount * parents, blank], axis=0).T
    back = jnp.zeros((all_blocks, 4 * slots), F32)
    for j in range(parents):
        pick = slot_row == item_rank[j:j + 1, :]
        spread = jnp.where(pick, scale[j:j + 1, :], 0.0)
        pad = jnp.zeros((slots, rows), BF16)
        stacked = jnp.concatenate(three(spread) + (pad,), axis=0)
        back = back + lax.dot_general(onehot[j], stacked, contract_last, preferred_element_type=F32)
    back = (back + pltpu.roll(back, 3 * slots, 1)) + pltpu.roll(back, 2 * slots, 1)
    for o in range(shards):
        back_out[o] = back[o * blocks:(o + 1) * blocks, :]
    back_in[0] = back_out[me]
    each(0, shards, lambda p: back_copy(p, holder(p), holder(p)).start())
    send_pay(CUTS[0], CUTS[1])
    each(0, shards, lambda p: back_copy(p, holder(p), holder(p)).wait_recv())
    lane8 = lax.broadcasted_iota(I32, (blocks, 128), 1)
    for t in range(shards // 4):
        joined = back_in[4 * t]
        for s in range(1, 4):
            joined = jnp.where(lane8 >= s * slots, pltpu.roll(back_in[4 * t + s], s * slots, 1), joined)
        sc[:, t * 128:(t + 1) * 128] = joined

    def sums(b):
        codes = et[b] * sc[pl.ds(b, 1), :]
        high = codes.astype(BF16)
        low = (codes - high.astype(F32)).astype(BF16)
        product = jnp.dot(jnp.concatenate([high, low], axis=0), g[b], preferred_element_type=F32)
        return product[:size] + product[size:], jnp.sum(codes, axis=1, keepdims=True)

    lane128 = lax.broadcasted_iota(I32, (size, 128), 1)
    column_scr[...] = jnp.zeros_like(column_scr)

    def sum_blocks(first, low, high):
        @pl.loop(low, high)
        def _(i):
            b = (2 * first + i) % blocks
            value, column = sums(b)
            part[b] = value
            column_scr[...] = jnp.where(lane128 == b, column, column_scr[...])

    def widen(low, high):
        @pl.loop(low, high)
        def _(o):
            here = pl.ds(pl.multiple_of(o * blocks * slots, blocks * slots), blocks * slots)
            wide[here, :] = ret_ref[o].astype(F32)

    def spread_rows(low, high):
        @pl.loop(low, high)
        def _(i):
            for r in range(16):
                for j in range(parents):
                    item = wide[pl.ds(slot_ref[j, i * 16 + r], 1), :]
                    code_rows[r:r + 1, j * size:(j + 1) * size] = item[:, :size]
                    deep_rows[r:r + 1, j * size:(j + 1) * size] = item[:, size:]
            here = pl.ds(pl.multiple_of(i * 16, 16), 16)
            low_rows = pl.ds(pl.multiple_of((i % 8) * 16, 16), 16)
            factors = scale_mass[here, :]
            for j in range(parents):
                part_j = slice(j * size, (j + 1) * size)
                g[0, here, part_j] = (code_rows[:, part_j] * factors[:, j:j + 1]).astype(BF16)
                part[i // 8, low_rows, part_j] = deep_rows[:, part_j] * factors[:, parents + j:parents + j + 1]

    def dp_copy(index, source_ref, target_ref, step):
        return pltpu.make_async_remote_copy(
            src_ref=source_ref, dst_ref=target_ref, send_sem=dp_send.at[index], recv_sem=dp_recv.at[index],
            device_id=((dp + step) % 4, me), device_id_type=MESH,
        )

    right, left, across = (dp + 1) % 4, (dp + 3) % 4, (dp + 2) % 4
    sum_blocks(across, 0, 2)
    own[0] = part[2 * across].astype(BF16)
    own[1] = part[2 * across + 1].astype(BF16)
    relay = [dp_copy(0, own.at[0], relay_in.at[0], 1), dp_copy(1, own.at[1], relay_in.at[1], 3)]
    for copy in relay:
        copy.start()
    send_pay(CUTS[1], CUTS[2])
    sum_blocks(across, 2, 4)
    sum_blocks(across, 6, 8)
    own[3] = part[2 * right + 1].astype(BF16)
    own[4] = part[2 * left].astype(BF16)
    near = [
        dp_copy(2, own.at[2], near_in.at[0], 1), dp_copy(3, own.at[3], near_in.at[1], 1),
        dp_copy(4, own.at[4], near_in.at[2], 3), dp_copy(5, own.at[5], near_in.at[3], 3),
    ]
    near[1].start()
    near[2].start()
    send_pay(CUTS[2], CUTS[3])
    sum_blocks(across, 4, 6)
    mass_send[...] = column_scr[...].T[0:blocks, :]
    mass_all[dp] = mass_send[...]
    mass_copies = [dp_copy(8 + d, mass_send, mass_all.at[dp], d) for d in (1, 2, 3)]
    for copy in mass_copies:
        copy.start()
    relay[0].wait_recv()
    own[2] = (part[2 * right] + relay_in[0].astype(F32)).astype(BF16)
    near[0].start()
    relay[1].wait_recv()
    own[5] = (part[2 * left + 1] + relay_in[1].astype(F32)).astype(BF16)
    near[3].start()
    send_pay(CUTS[3], shards)
    for copy in mass_copies:
        copy.wait_recv()
    all_mass = ((mass_all[0] + mass_all[1]) + mass_all[2]) + mass_all[3]
    total_ref[...] = all_mass
    spare = jnp.zeros((128 - blocks, 128), F32)
    column_scr[...] = jnp.maximum(jnp.concatenate([all_mass, spare], axis=0), 1.0).T
    for copy in near:
        copy.wait_recv()
    for i in range(2):
        b = 2 * dp + i
        column = jnp.sum(jnp.where(lane128 == b, column_scr[...], 0.0), axis=1, keepdims=True)
        value = part[b] + (near_in[i].astype(F32) + near_in[2 + i].astype(F32))
        own[6 + i] = (value / column).astype(BF16)
    ready = [
        dp_copy(12, own.at[6], fin_ref.at[2 * dp], 1), dp_copy(13, own.at[7], fin_ref.at[2 * dp + 1], 3),
        dp_copy(14, own.at[7], fin_ref.at[2 * dp + 1], 1), dp_copy(15, own.at[6], fin_ref.at[2 * dp], 3),
    ]
    for copy in ready:
        copy.start()
    own_fin = [pltpu.make_async_copy(own.at[6 + i], fin_ref.at[2 * dp + i], local_sem.at[2 + i]) for i in range(2)]
    for copy in own_fin:
        copy.start()
    dp_copy(12, own.at[6], fin_ref.at[2 * left], 1).wait_recv()
    onward = [dp_copy(6, fin_ref.at[2 * left], fin_ref.at[2 * left], 1)]
    onward[0].start()
    dp_copy(13, own.at[7], fin_ref.at[2 * right + 1], 3).wait_recv()
    onward.append(dp_copy(7, fin_ref.at[2 * right + 1], fin_ref.at[2 * right + 1], 3))
    onward[1].start()
    each(0, shards, lambda p: pay_copy(p, holder(p), source(p)).wait_recv())
    own_pay.wait()
    widen(0, shards)
    steps = rows // 16
    spread_rows(0, steps)
    outs = [pltpu.make_async_copy(g.at[0, pl.ds(0, rows), :], codes_ref, out_sem.at[4])]
    for i in range(rows // size):
        outs.append(pltpu.make_async_copy(part.at[i], deeper_ref.at[pl.ds(i * size, size), :], out_sem.at[i]))
    for copy in outs:
        copy.start()
    dp_copy(14, own.at[7], fin_ref.at[2 * left + 1], 1).wait_recv()
    dp_copy(15, own.at[6], fin_ref.at[2 * right], 3).wait_recv()
    dp_copy(6, own.at[6], fin_ref.at[2 * across], 1).wait_recv()
    dp_copy(7, own.at[7], fin_ref.at[2 * across + 1], 3).wait_recv()

    for copy in sent + mass_copies + relay + near + ready + onward:
        copy.wait_send()
    each(0, shards, lambda p: pay_copy(p, me, source(p)).wait_send())
    each(0, shards, lambda p: stat_copy(p, me, source(p)).wait_send())
    each(0, shards, lambda p: back_copy(p, holder(p), holder(p)).wait_send())
    for copy in own_fin + outs:
        copy.wait()


def params():
    return pltpu.CompilerParams(vmem_limit_bytes=VMEM_LIMIT)


def body(embeddings, parents, children, temper, level_two, level_three):
    rows, depth = embeddings.shape
    count = parents.shape[1]
    blocks = temper.shape[0]
    size = level_two.shape[0] // blocks
    kinds = level_three.shape[0] // (blocks * size)
    shards = lax.axis_size("clus")
    all_blocks = blocks * shards
    slots = 2 * rows * count // all_blocks
    assert kinds == 2 and shards == 32 and slots == 32 and blocks == 8 and lax.axis_size("dp") == 4

    packed = (parents * kinds + children).T
    total_rows = rows + 2 * count
    extended, place = pl.pallas_call(
        functools.partial(prepare_kernel, all_blocks, slots),
        out_shape=[jax.ShapeDtypeStruct((total_rows, depth), BF16), jax.ShapeDtypeStruct((count, rows), I32)],
        compiler_params=params(),
    )(packed, embeddings)
    anywhere = pl.BlockSpec(memory_space=pl.ANY)
    vmem = pl.BlockSpec(memory_space=pltpu.VMEM)
    dma = pltpu.SemaphoreType.DMA

    _, sums, cluster_mass, soft_codes, candidate_scores = pl.pallas_call(
        fused_kernel,
        in_specs=[
            pl.BlockSpec(memory_space=pltpu.SMEM), pl.BlockSpec(memory_space=pltpu.SMEM),
            anywhere, vmem, anywhere, anywhere,
        ],
        out_specs=[anywhere, anywhere, vmem, anywhere, anywhere],
        out_shape=[
            jax.ShapeDtypeStruct((shards, total_rows, depth), BF16),
            jax.ShapeDtypeStruct((blocks, size, depth), BF16),
            jax.ShapeDtypeStruct((blocks, size), F32),
            jax.ShapeDtypeStruct((rows, count * size), BF16),
            jax.ShapeDtypeStruct((rows, count * size), F32),
        ],
        scratch_shapes=[
            pltpu.VMEM((4, total_rows, depth), BF16),
            pltpu.VMEM(level_two.shape, BF16),
            pltpu.VMEM(level_three.shape, BF16),
            pltpu.VMEM((blocks, shards * slots, depth), BF16),
            pltpu.VMEM((blocks, size, shards * slots), F32),
            pltpu.VMEM((shards, blocks * slots, 2 * size), BF16),
            pltpu.VMEM((shards * slots, 128), F32),
            pltpu.VMEM((rows, rows), BF16),
            pltpu.VMEM((shards * slots, 128), F32),
            pltpu.VMEM((shards, 2 * blocks, 128), F32),
            pltpu.VMEM((shards, 2 * blocks, 128), F32),
            pltpu.VMEM((count, all_blocks, rows), BF16),
            pltpu.VMEM((count, rows), F32),
            pltpu.VMEM((shards, blocks, 128), F32),
            pltpu.VMEM((shards, blocks, 128), F32),
            pltpu.VMEM((blocks, shards * slots), F32),
            pltpu.VMEM((blocks, size, depth), F32),
            pltpu.VMEM((2, size, depth), BF16),
            pltpu.VMEM((4, size, depth), BF16),
            pltpu.VMEM((8, size, depth), BF16),
            pltpu.VMEM((4, blocks, 128), F32),
            pltpu.VMEM((blocks, 128), F32),
            pltpu.VMEM((size, 128), F32),
            pltpu.VMEM((shards, blocks * slots, 2 * size), BF16),
            pltpu.VMEM((shards * blocks * slots, 2 * size), F32),
            pltpu.VMEM((rows, 128), F32),
            pltpu.VMEM((16, count * size), F32),
            pltpu.VMEM((16, count * size), F32),
            dma((5,)),
            dma((4,)), dma((2,)), dma((4,)), dma((40,)), dma((40,)), dma((32,)), dma((32,)),
            dma((shards,)), dma((shards,)), dma((shards,)), dma((shards,)), dma((shards,)), dma((shards,)),
            dma((16,)), dma((16,)),
        ],
        compiler_params=pltpu.CompilerParams(
            vmem_limit_bytes=VMEM_LIMIT, collective_id=0, has_side_effects=True
        ),
    )(temper, place, extended, place, level_two, level_three)

    new_centroids = sums.reshape(blocks * size, depth).astype(F32)
    return soft_codes, candidate_scores, new_centroids, cluster_mass.reshape(blocks * size)


def solution(mesh):
    rows = P(("dp", "clus"), None)
    return jax.shard_map(
        body,
        mesh=mesh,
        in_specs=(rows, rows, rows, P("clus"), P("clus", None), P("clus", None)),
        out_specs=(rows, rows, P("clus", None), P("clus")),
        check_vma=False,
    )
```

```python
import functools

import jax
import jax.numpy as jnp
from jax import lax
from jax.experimental import pallas as pl
from jax.experimental.pallas import tpu as pltpu
from jax.sharding import PartitionSpec as P

F32, BF16, I32 = jnp.float32, jnp.bfloat16, jnp.int32
MESH = pl.DeviceIdType.MESH
VMEM_LIMIT = 62 << 20

ORDER = (
    (0, 0), (1, 0), (0, 1), (3, 0), (0, 3), (1, 1), (1, 3), (3, 1),
    (3, 3), (2, 0), (0, 2), (2, 1), (1, 2), (2, 3), (3, 2), (2, 2),
)
WAVES = (0, 12, 24, 32)
CUTS = (18, 22, 26, 30)
RING = (0, 1, 3, 2)


def packed_table(values):
    word = sum(v << (2 * i) for i, v in enumerate(values))
    return word - (1 << 32) if word >= 1 << 31 else word


TABLE_Y = packed_table([o[0] for o in ORDER])
TABLE_Z = packed_table([o[1] for o in ORDER])


def entry(table, index):
    return lax.shift_right_logical(jnp.int32(table), jnp.int32(2) * index) % 4


def strict_upper(size):
    row = lax.broadcasted_iota(I32, (size, size), 0)
    column = lax.broadcasted_iota(I32, (size, size), 1)
    return jnp.where(row < column, 1.0, 0.0).astype(BF16)


def three(x):
    high = x.astype(BF16)
    rest = x - high.astype(F32)
    middle = rest.astype(BF16)
    low = (rest - middle.astype(F32)).astype(BF16)
    return high, middle, low


def prepare_kernel(all_blocks, slots, packed_ref, rows_ref, ext_ref, slot_ref):
    parents, rows = packed_ref.shape
    depth = rows_ref.shape[1]
    named = lax.shift_right_logical(packed_ref[...], 1)
    kind = packed_ref[...] & 1
    ids = jnp.concatenate([named.astype(F32), kind.astype(F32)], axis=0).astype(BF16)
    ext_ref[0:2 * parents, 0:rows] = ids
    ext_ref[0:2 * parents, rows:depth] = jnp.zeros((2 * parents, depth - rows), BF16)
    ext_ref[2 * parents:2 * parents + rows, :] = rows_ref[...]
    number = lax.broadcasted_iota(I32, (all_blocks, rows), 0)
    hit = jnp.zeros((all_blocks, rows), F32)
    for j in range(parents):
        hit = hit + jnp.where(named[j:j + 1] == number, 1.0, 0.0)
    rank = jnp.dot(hit.astype(BF16), strict_upper(rows), preferred_element_type=F32)
    for j in range(parents):
        own = jnp.sum(jnp.where(named[j:j + 1] == number, rank, 0.0), axis=0, keepdims=True)
        slot_ref[j:j + 1, :] = named[j:j + 1] * slots + own.astype(I32)


def fused_kernel(
    temper_ref, slot_ref, ext_ref, place_ref, two_ref, three_ref,
    buf_ref, fin_ref, total_ref, codes_ref, deeper_ref,
    rowbuf, w2, w3, g, et, pay, child, upper, stats, stat_out, stat_in, onehot, item_rank, back_out, back_in,
    sc, part, relay_in, near_in, own, mass_all, mass_send, column_scr,
    ret_ref, wide, scale_mass, code_rows, deep_rows, out_sem,
    load_sem, w_sem, local_sem, ring_send, ring_recv, sib_send, sib_recv, pay_send, pay_recv,
    stat_send, stat_recv, back_send, back_recv, dp_send, dp_recv,
):
    parents, rows = place_ref.shape
    total_rows, depth = ext_ref.shape
    slots = 32
    blocks = temper_ref.shape[0]
    size = w2.shape[0] // blocks
    shards = buf_ref.shape[0]
    all_blocks = blocks * shards
    dp = lax.axis_index("dp")
    me = lax.axis_index("clus")
    core = me % 2
    z = (me // 2) % 4
    y = me // 8
    sibling = me + 1 - 2 * core

    def at(dy, dz, flip=0):
        return (((y + dy) % 4) * 4 + (z + dz) % 4) * 2 + (core + flip) % 2

    def source(p):
        q = p // 2
        return at(entry(TABLE_Y, q), entry(TABLE_Z, q), p % 2)

    def holder(p):
        q = p // 2
        return at(4 - entry(TABLE_Y, q), 4 - entry(TABLE_Z, q), p % 2)

    barrier = pltpu.get_barrier_semaphore()

    @pl.loop(1, shards)
    def _(d):
        pl.semaphore_signal(barrier, inc=1, device_id=(dp, (me + d) % shards), device_id_type=MESH)

    for d in (1, 2, 3):
        pl.semaphore_signal(barrier, inc=1, device_id=((dp + d) % 4, me), device_id_type=MESH)
    pl.semaphore_wait(barrier, shards - 1 + 3)

    quarter = rows // 4
    ids = total_rows - rows
    piece = {
        "A": (0, ids + 2 * quarter), "A0": (0, ids + quarter), "A1": (ids + quarter, quarter),
        "B": (ids + 2 * quarter, 2 * quarter), "B0": (ids + 2 * quarter, quarter), "B1": (ids + 3 * quarter, quarter),
    }

    def part_of(ref, name):
        start, length = piece[name]
        return ref.at[pl.ds(start, length), :]

    def chip(half, first, second):
        return (first, second) if half == "A" else (second, first)

    def ring(half, k, offset, name, step):
        index = (0 if half == "A" else 20) + k
        block = at(*offset)
        mine = ext_ref if offset == (0, 0) else buf_ref.at[block]
        return pltpu.make_async_remote_copy(
            src_ref=part_of(mine, name), dst_ref=part_of(buf_ref.at[block], name),
            send_sem=ring_send.at[index], recv_sem=ring_recv.at[index],
            device_id=(dp, at(*step)), device_id_type=MESH,
        )

    def arrival(half, k, offset, name):
        index = (0 if half == "A" else 20) + k
        block = at(*offset)
        return pltpu.make_async_remote_copy(
            src_ref=part_of(buf_ref.at[block], name), dst_ref=part_of(buf_ref.at[block], name),
            send_sem=ring_send.at[index], recv_sem=ring_recv.at[index],
            device_id=(dp, at(1, 0)), device_id_type=MESH,
        )

    sent = []

    def go(copy):
        copy.start()
        sent.append(copy)

    def share(half, offset):
        index = (0 if half == "A" else 16) + ORDER.index(offset)
        block = at(*offset)
        mine = ext_ref if offset == (0, 0) else buf_ref.at[block]
        go(pltpu.make_async_remote_copy(
            src_ref=part_of(mine, half), dst_ref=part_of(buf_ref.at[block], half),
            send_sem=sib_send.at[index], recv_sem=sib_recv.at[index],
            device_id=(dp, sibling), device_id_type=MESH,
        ))

    def shared(half, q):
        index = (0 if half == "A" else 16) + q
        block = at(*ORDER[q], 1)
        pltpu.make_async_remote_copy(
            src_ref=part_of(buf_ref.at[block], half), dst_ref=part_of(buf_ref.at[block], half),
            send_sem=sib_send.at[index], recv_sem=sib_recv.at[index],
            device_id=(dp, sibling), device_id_type=MESH,
        ).wait_recv()

    def first_axis(half, step):
        return chip(half, step, 0)

    def second_axis(half, step):
        return chip(half, 0, step)

    def enter_second(half, i):
        block = chip(half, RING[i], 0)
        go(ring(half, 4 + 4 * i, block, half, second_axis(half, 1)))
        go(ring(half, 5 + 4 * i, block, half, second_axis(half, 3)))

    def first_near(half):
        arrival(half, 1, chip(half, 1, 0), half).wait_recv()
        go(ring(half, 3, chip(half, 1, 0), half + "1", first_axis(half, 3)))
        arrival(half, 0, chip(half, 3, 0), half).wait_recv()
        go(ring(half, 2, chip(half, 3, 0), half + "0", first_axis(half, 1)))

    def first_near_on(half):
        enter_second(half, 1)
        enter_second(half, 2)
        share(half, chip(half, 1, 0))
        share(half, chip(half, 3, 0))

    def first_far(half):
        arrival(half, 2, chip(half, 2, 0), half + "0").wait_recv()
        arrival(half, 3, chip(half, 2, 0), half + "1").wait_recv()
        enter_second(half, 3)
        share(half, chip(half, 2, 0))

    def second_near(half, i):
        o = RING[i]
        arrival(half, 5 + 4 * i, chip(half, o, 1), half).wait_recv()
        go(ring(half, 7 + 4 * i, chip(half, o, 1), half + "1", second_axis(half, 3)))
        arrival(half, 4 + 4 * i, chip(half, o, 3), half).wait_recv()
        go(ring(half, 6 + 4 * i, chip(half, o, 3), half + "0", second_axis(half, 1)))
        share(half, chip(half, o, 1))
        share(half, chip(half, o, 3))

    def second_far(half, i):
        o = RING[i]
        arrival(half, 6 + 4 * i, chip(half, o, 2), half + "0").wait_recv()
        arrival(half, 7 + 4 * i, chip(half, o, 2), half + "1").wait_recv()
        share(half, chip(half, o, 2))

    def load(p):
        return pltpu.make_async_copy(buf_ref.at[source(p)], rowbuf.at[p % 4], load_sem.at[p % 4])

    first_block = (me * blocks).astype(F32)

    def pay_copy(p, index, device):
        return pltpu.make_async_remote_copy(
            src_ref=pay.at[p], dst_ref=ret_ref.at[index], send_sem=pay_send.at[p], recv_sem=pay_recv.at[p],
            device_id=(dp, device), device_id_type=MESH,
        )

    def place_of(k):
        return (k // 8) * 8 + (k % 4) * 2 + (k % 8) // 4

    def start_pay(k):
        p = place_of(k)
        pay_copy(p, me, source(p)).start()

    def gather(low, high, send=None):
        for q in range(low // 2, high // 2):
            shared("A", q)
            shared("B", q)
        for p in range(low, min(low + 3, high)):
            load(jnp.int32(p)).start()
        slot_id = lax.broadcasted_iota(I32, (slots, rows), 0).astype(F32)
        lane = lax.broadcasted_iota(I32, (slots, 128), 1)

        @pl.loop(low, high)
        def _(p):
            load(p).wait()
            if send is not None:
                start_pay(p + (send - low))

            @pl.when(p + 3 < high)
            def _():
                load(p + 3).start()

            meta = rowbuf[p % 4, 0:2 * parents, 0:rows].astype(F32)
            block = meta[:parents] - first_block
            kind = meta[parents:]
            hits, kinds = [], []
            for b in range(blocks):
                match = block == float(b)
                hits.append(jnp.sum(jnp.where(match, 1.0, 0.0), axis=0, keepdims=True))
                kinds.append(jnp.sum(jnp.where(match, kind, 0.0), axis=0, keepdims=True))
            hit = jnp.concatenate(hits, axis=0)
            rank = jnp.dot(hit.astype(BF16), upper[...], preferred_element_type=F32)
            rank = jnp.where(hit > 0.0, rank, -1.0)
            selects = []
            child_lanes = jnp.zeros((slots, 128), F32)
            for b in range(blocks):
                select = slot_id == rank[b:b + 1]
                column = jnp.sum(jnp.where(select, kinds[b], 0.0), axis=1, keepdims=True)
                child_lanes = jnp.where(lane == b, column, child_lanes)
                selects.append(jnp.where(select, 1.0, 0.0).astype(BF16))
            select = jnp.concatenate(selects, axis=0)
            picked = jnp.dot(
                select, rowbuf[p % 4, ids:total_rows, :], preferred_element_type=F32
            ).astype(BF16)
            place = pl.ds(pl.multiple_of(p * slots, slots), slots)
            child[place, :] = child_lanes
            for b in range(blocks):
                g[b, place, :] = picked[b * slots:(b + 1) * slots]

    contract_last = (((1,), (1,)), ((), ()))

    def score(wave, low, high, send=None):
        start, count = WAVES[wave] * slots, (WAVES[wave + 1] - WAVES[wave]) * slots
        here = slice(start, start + count)
        lane = lax.broadcasted_iota(I32, (count, 128), 1)

        @pl.loop(low, high)
        def _(b):
            if send is not None:
                @pl.when(b % 2 == 0)
                def _():
                    start_pay(b // 2 + send)

            x = g[b, here, :]
            near = lax.dot_general(
                x, w2[pl.ds(pl.multiple_of(b * size, size), size), :], contract_last, preferred_element_type=F32
            )
            far = lax.dot_general(
                x, w3[pl.ds(pl.multiple_of(b * 2 * size, 2 * size), 2 * size), :], contract_last,
                preferred_element_type=F32,
            )
            value = near * temper_ref[b]
            which = jnp.sum(jnp.where(lane == b, child[here, :], 0.0), axis=1, keepdims=True)
            deeper = jnp.where(which > 0.5, far[:, size:], far[:, :size]).astype(BF16)
            most = jnp.max(value, axis=1, keepdims=True)
            weight = jnp.exp(value - most)
            amount = jnp.sum(weight, axis=1, keepdims=True)
            old = stats[here, :]
            stats[here, :] = jnp.where(lane == b, most, jnp.where(lane == b + blocks, amount, old))
            et[b, :, here] = weight.T
            weight = weight.astype(BF16)
            place = pl.ds(pl.multiple_of(b * slots, slots), slots)
            for i in range(count // slots):
                pay[WAVES[wave] + i, place, 0:size] = weight[i * slots:(i + 1) * slots]
                pay[WAVES[wave] + i, place, size:2 * size] = deeper[i * slots:(i + 1) * slots]

    def each(low, high, action):
        @pl.loop(max(low, 1), high)
        def _(p):
            action(p)

    def stat_copy(p, index, device):
        return pltpu.make_async_remote_copy(
            src_ref=stat_out.at[p], dst_ref=stat_in.at[index], send_sem=stat_send.at[p], recv_sem=stat_recv.at[p],
            device_id=(dp, device), device_id_type=MESH,
        )

    def send_stats(wave):
        low, high = WAVES[wave], WAVES[wave + 1]
        for t in range(low // 4, high // 4):
            flipped = stats[t * 128:(t + 1) * 128, :].T[0:2 * blocks, :]
            for s in range(4):
                moved = flipped if s == 0 else pltpu.roll(flipped, 128 - s * slots, 1)
                stat_out[t * 4 + s] = moved
        if low == 0:
            stat_in[me] = stat_out[0]
        each(low, high, lambda p: stat_copy(p, me, source(p)).start())

    def send_pay(low, high):
        each(low, high, start_pay)

    def back_copy(p, index, device):
        return pltpu.make_async_remote_copy(
            src_ref=back_out.at[index], dst_ref=back_in.at[p], send_sem=back_send.at[p], recv_sem=back_recv.at[p],
            device_id=(dp, device), device_id_type=MESH,
        )

    for half, step in (("A", 1), ("B", 1)):
        go(ring(half, 0, (0, 0), half, first_axis(half, 1)))
        go(ring(half, 1, (0, 0), half, first_axis(half, 3)))
    enter_second("A", 0)
    enter_second("B", 0)
    share("A", (0, 0))
    share("B", (0, 0))
    in_two = pltpu.make_async_copy(two_ref, w2, w_sem.at[0])
    in_three = pltpu.make_async_copy(three_ref, w3, w_sem.at[1])
    in_two.start()
    in_three.start()
    own_in = pltpu.make_async_copy(ext_ref, rowbuf.at[0], local_sem.at[0])
    own_in.start()
    upper[...] = strict_upper(rows)
    stats[...] = jnp.zeros_like(stats)
    back_out[...] = jnp.zeros_like(back_out)
    own_in.wait()
    own_out = pltpu.make_async_copy(rowbuf.at[0], buf_ref.at[me], local_sem.at[1])
    own_out.start()

    named = lax.shift_right_logical(place_ref[...], 5)
    item_rank[...] = (place_ref[...] & (slots - 1)).astype(F32)
    number = lax.broadcasted_iota(I32, (all_blocks, rows), 0)
    for j in range(parents):
        onehot[j] = jnp.where(named[j:j + 1] == number, 1.0, 0.0).astype(BF16)
    own_out.wait()

    first_near("A")
    first_near("B")
    first_near_on("A")
    first_near_on("B")
    gather(0, 2)
    second_near("A", 0)
    second_near("B", 0)
    first_far("A")
    first_far("B")
    gather(2, 10)
    second_near("A", 1)
    second_near("B", 1)
    gather(10, 12)
    in_two.wait()
    in_three.wait()
    score(0, 0, blocks)
    second_near("A", 2)
    second_near("B", 2)
    send_stats(0)
    gather(12, 18)
    second_far("A", 0)
    second_far("B", 0)
    gather(18, 22)
    second_near("A", 3)
    second_near("B", 3)
    second_far("A", 1)
    second_far("B", 1)
    gather(22, 26, 1)
    score(1, 0, blocks)
    second_far("A", 2)
    second_far("B", 2)
    second_far("A", 3)
    second_far("B", 3)
    send_stats(1)
    gather(26, 32, 5)
    score(2, 0, blocks, 11)
    send_stats(2)
    send_pay(15, CUTS[0])
    own_pay = pltpu.make_async_copy(pay.at[0], ret_ref.at[me], local_sem.at[0])
    own_pay.start()

    each(0, shards, lambda p: stat_copy(p, holder(p), source(p)).wait_recv())
    table = jnp.concatenate([stat_in[o, 0:blocks, :] for o in range(shards)], axis=0)
    table_sum = jnp.concatenate([stat_in[o, blocks:2 * blocks, :] for o in range(shards)], axis=0)
    both = jnp.concatenate([table.T[0:slots], table_sum.T[0:slots]], axis=0)
    stack = jnp.concatenate(three(both), axis=0)
    slot_row = lax.broadcasted_iota(I32, (slots, rows), 0).astype(F32)
    mosts, amounts = [], []
    for j in range(parents):
        found = jnp.dot(stack, onehot[j], preferred_element_type=F32)
        found = (found[0:2 * slots] + found[2 * slots:4 * slots]) + found[4 * slots:6 * slots]
        pick = slot_row == item_rank[j:j + 1, :]
        mosts.append(jnp.sum(jnp.where(pick, found[0:slots], 0.0), axis=0, keepdims=True))
        amounts.append(jnp.sum(jnp.where(pick, found[slots:], 0.0), axis=0, keepdims=True))
    most = jnp.concatenate(mosts, axis=0)
    amount = jnp.concatenate(amounts, axis=0)
    weight = jnp.exp(most - jnp.max(most, axis=0, keepdims=True))
    scale = weight / jnp.sum(weight * amount, axis=0, keepdims=True)
    blank = jnp.zeros((128 - 2 * parents, rows), F32)
    scale_mass[...] = jnp.concatenate([scale, scale * amount * parents, blank], axis=0).T
    back = jnp.zeros((all_blocks, 4 * slots), F32)
    for j in range(parents):
        pick = slot_row == item_rank[j:j + 1, :]
        spread = jnp.where(pick, scale[j:j + 1, :], 0.0)
        pad = jnp.zeros((slots, rows), BF16)
        stacked = jnp.concatenate(three(spread) + (pad,), axis=0)
        back = back + lax.dot_general(onehot[j], stacked, contract_last, preferred_element_type=F32)
    back = (back + pltpu.roll(back, 3 * slots, 1)) + pltpu.roll(back, 2 * slots, 1)
    for o in range(shards):
        back_out[o] = back[o * blocks:(o + 1) * blocks, :]
    back_in[0] = back_out[me]
    each(0, shards, lambda p: back_copy(p, holder(p), holder(p)).start())
    send_pay(CUTS[0], CUTS[1])
    each(0, shards, lambda p: back_copy(p, holder(p), holder(p)).wait_recv())
    lane8 = lax.broadcasted_iota(I32, (blocks, 128), 1)
    for t in range(shards // 4):
        joined = back_in[4 * t]
        for s in range(1, 4):
            joined = jnp.where(lane8 >= s * slots, pltpu.roll(back_in[4 * t + s], s * slots, 1), joined)
        sc[:, t * 128:(t + 1) * 128] = joined

    def sums(b):
        codes = et[b] * sc[pl.ds(b, 1), :]
        high = codes.astype(BF16)
        low = (codes - high.astype(F32)).astype(BF16)
        product = jnp.dot(jnp.concatenate([high, low], axis=0), g[b], preferred_element_type=F32)
        return product[:size] + product[size:], jnp.sum(codes, axis=1, keepdims=True)

    lane128 = lax.broadcasted_iota(I32, (size, 128), 1)
    column_scr[...] = jnp.zeros_like(column_scr)

    def sum_blocks(first, low, high):
        @pl.loop(low, high)
        def _(i):
            b = (2 * first + i) % blocks
            value, column = sums(b)
            part[b] = value
            column_scr[...] = jnp.where(lane128 == b, column, column_scr[...])

    def widen_arrived():
        @pl.loop(0, shards)
        def _(k):
            p = place_of(k)

            @pl.when(k > 0)
            def _():
                pay_copy(p, holder(p), source(p)).wait_recv()

            o = holder(p)
            here = pl.ds(pl.multiple_of(o * (blocks * slots), blocks * slots), blocks * slots)
            wide[here, :] = ret_ref[o].astype(F32)

    def spread_rows(low, high):
        @pl.loop(low, high)
        def _(i):
            for r in range(16):
                for j in range(parents):
                    item = wide[pl.ds(slot_ref[j, i * 16 + r], 1), :]
                    code_rows[r:r + 1, j * size:(j + 1) * size] = item[:, :size]
                    deep_rows[r:r + 1, j * size:(j + 1) * size] = item[:, size:]
            here = pl.ds(pl.multiple_of(i * 16, 16), 16)
            low_rows = pl.ds(pl.multiple_of((i % 8) * 16, 16), 16)
            factors = scale_mass[here, :]
            for j in range(parents):
                part_j = slice(j * size, (j + 1) * size)
                g[0, here, part_j] = (code_rows[:, part_j] * factors[:, j:j + 1]).astype(BF16)
                part[i // 8, low_rows, part_j] = deep_rows[:, part_j] * factors[:, parents + j:parents + j + 1]

    def dp_copy(index, source_ref, target_ref, step):
        return pltpu.make_async_remote_copy(
            src_ref=source_ref, dst_ref=target_ref, send_sem=dp_send.at[index], recv_sem=dp_recv.at[index],
            device_id=((dp + step) % 4, me), device_id_type=MESH,
        )

    right, left, across = (dp + 1) % 4, (dp + 3) % 4, (dp + 2) % 4
    sum_blocks(across, 0, 2)
    own[0] = part[2 * across].astype(BF16)
    own[1] = part[2 * across + 1].astype(BF16)
    relay = [dp_copy(0, own.at[0], relay_in.at[0], 1), dp_copy(1, own.at[1], relay_in.at[1], 3)]
    for copy in relay:
        copy.start()
    send_pay(CUTS[1], CUTS[2])
    sum_blocks(across, 2, 4)
    sum_blocks(across, 6, 8)
    own[3] = part[2 * right + 1].astype(BF16)
    own[4] = part[2 * left].astype(BF16)
    near = [
        dp_copy(2, own.at[2], near_in.at[0], 1), dp_copy(3, own.at[3], near_in.at[1], 1),
        dp_copy(4, own.at[4], near_in.at[2], 3), dp_copy(5, own.at[5], near_in.at[3], 3),
    ]
    near[1].start()
    near[2].start()
    send_pay(CUTS[2], CUTS[3])
    sum_blocks(across, 4, 6)
    mass_send[...] = column_scr[...].T[0:blocks, :]
    mass_all[dp] = mass_send[...]
    mass_copies = [dp_copy(8 + d, mass_send, mass_all.at[dp], d) for d in (1, 2, 3)]
    for copy in mass_copies:
        copy.start()
    relay[0].wait_recv()
    own[2] = (part[2 * right] + relay_in[0].astype(F32)).astype(BF16)
    near[0].start()
    relay[1].wait_recv()
    own[5] = (part[2 * left + 1] + relay_in[1].astype(F32)).astype(BF16)
    near[3].start()
    send_pay(CUTS[3], shards)
    for copy in mass_copies:
        copy.wait_recv()
    all_mass = ((mass_all[0] + mass_all[1]) + mass_all[2]) + mass_all[3]
    total_ref[...] = all_mass
    spare = jnp.zeros((128 - blocks, 128), F32)
    column_scr[...] = jnp.maximum(jnp.concatenate([all_mass, spare], axis=0), 1.0).T
    for copy in near:
        copy.wait_recv()
    for i in range(2):
        b = 2 * dp + i
        column = jnp.sum(jnp.where(lane128 == b, column_scr[...], 0.0), axis=1, keepdims=True)
        value = part[b] + (near_in[i].astype(F32) + near_in[2 + i].astype(F32))
        own[6 + i] = (value / column).astype(BF16)
    ready = [
        dp_copy(12, own.at[6], fin_ref.at[2 * dp], 1), dp_copy(13, own.at[7], fin_ref.at[2 * dp + 1], 3),
        dp_copy(14, own.at[7], fin_ref.at[2 * dp + 1], 1), dp_copy(15, own.at[6], fin_ref.at[2 * dp], 3),
    ]
    for copy in ready:
        copy.start()
    own_fin = [pltpu.make_async_copy(own.at[6 + i], fin_ref.at[2 * dp + i], local_sem.at[2 + i]) for i in range(2)]
    for copy in own_fin:
        copy.start()
    dp_copy(12, own.at[6], fin_ref.at[2 * left], 1).wait_recv()
    onward = [dp_copy(6, fin_ref.at[2 * left], fin_ref.at[2 * left], 1)]
    onward[0].start()
    dp_copy(13, own.at[7], fin_ref.at[2 * right + 1], 3).wait_recv()
    onward.append(dp_copy(7, fin_ref.at[2 * right + 1], fin_ref.at[2 * right + 1], 3))
    onward[1].start()
    own_pay.wait()
    widen_arrived()
    steps = rows // 16
    spread_rows(0, steps)
    outs = [pltpu.make_async_copy(g.at[0, pl.ds(0, rows), :], codes_ref, out_sem.at[4])]
    for i in range(rows // size):
        outs.append(pltpu.make_async_copy(part.at[i], deeper_ref.at[pl.ds(i * size, size), :], out_sem.at[i]))
    for copy in outs:
        copy.start()
    dp_copy(14, own.at[7], fin_ref.at[2 * left + 1], 1).wait_recv()
    dp_copy(15, own.at[6], fin_ref.at[2 * right], 3).wait_recv()
    dp_copy(6, own.at[6], fin_ref.at[2 * across], 1).wait_recv()
    dp_copy(7, own.at[7], fin_ref.at[2 * across + 1], 3).wait_recv()

    for copy in sent + mass_copies + relay + near + ready + onward:
        copy.wait_send()
    each(0, shards, lambda p: pay_copy(p, me, source(p)).wait_send())
    each(0, shards, lambda p: stat_copy(p, me, source(p)).wait_send())
    each(0, shards, lambda p: back_copy(p, holder(p), holder(p)).wait_send())
    for copy in own_fin + outs:
        copy.wait()


def params():
    return pltpu.CompilerParams(vmem_limit_bytes=VMEM_LIMIT)


def body(embeddings, parents, children, temper, level_two, level_three):
    rows, depth = embeddings.shape
    count = parents.shape[1]
    blocks = temper.shape[0]
    size = level_two.shape[0] // blocks
    kinds = level_three.shape[0] // (blocks * size)
    shards = lax.axis_size("clus")
    all_blocks = blocks * shards
    slots = 2 * rows * count // all_blocks
    assert kinds == 2 and shards == 32 and slots == 32 and blocks == 8 and lax.axis_size("dp") == 4

    packed = (parents * kinds + children).T
    total_rows = rows + 2 * count
    extended, place = pl.pallas_call(
        functools.partial(prepare_kernel, all_blocks, slots),
        out_shape=[jax.ShapeDtypeStruct((total_rows, depth), BF16), jax.ShapeDtypeStruct((count, rows), I32)],
        compiler_params=params(),
    )(packed, embeddings)
    anywhere = pl.BlockSpec(memory_space=pl.ANY)
    vmem = pl.BlockSpec(memory_space=pltpu.VMEM)
    dma = pltpu.SemaphoreType.DMA

    _, sums, cluster_mass, soft_codes, candidate_scores = pl.pallas_call(
        fused_kernel,
        in_specs=[
            pl.BlockSpec(memory_space=pltpu.SMEM), pl.BlockSpec(memory_space=pltpu.SMEM),
            anywhere, vmem, anywhere, anywhere,
        ],
        out_specs=[anywhere, anywhere, vmem, anywhere, anywhere],
        out_shape=[
            jax.ShapeDtypeStruct((shards, total_rows, depth), BF16),
            jax.ShapeDtypeStruct((blocks, size, depth), BF16),
            jax.ShapeDtypeStruct((blocks, size), F32),
            jax.ShapeDtypeStruct((rows, count * size), BF16),
            jax.ShapeDtypeStruct((rows, count * size), F32),
        ],
        scratch_shapes=[
            pltpu.VMEM((4, total_rows, depth), BF16),
            pltpu.VMEM(level_two.shape, BF16),
            pltpu.VMEM(level_three.shape, BF16),
            pltpu.VMEM((blocks, shards * slots, depth), BF16),
            pltpu.VMEM((blocks, size, shards * slots), F32),
            pltpu.VMEM((shards, blocks * slots, 2 * size), BF16),
            pltpu.VMEM((shards * slots, 128), F32),
            pltpu.VMEM((rows, rows), BF16),
            pltpu.VMEM((shards * slots, 128), F32),
            pltpu.VMEM((shards, 2 * blocks, 128), F32),
            pltpu.VMEM((shards, 2 * blocks, 128), F32),
            pltpu.VMEM((count, all_blocks, rows), BF16),
            pltpu.VMEM((count, rows), F32),
            pltpu.VMEM((shards, blocks, 128), F32),
            pltpu.VMEM((shards, blocks, 128), F32),
            pltpu.VMEM((blocks, shards * slots), F32),
            pltpu.VMEM((blocks, size, depth), F32),
            pltpu.VMEM((2, size, depth), BF16),
            pltpu.VMEM((4, size, depth), BF16),
            pltpu.VMEM((8, size, depth), BF16),
            pltpu.VMEM((4, blocks, 128), F32),
            pltpu.VMEM((blocks, 128), F32),
            pltpu.VMEM((size, 128), F32),
            pltpu.VMEM((shards, blocks * slots, 2 * size), BF16),
            pltpu.VMEM((shards * blocks * slots, 2 * size), F32),
            pltpu.VMEM((rows, 128), F32),
            pltpu.VMEM((16, count * size), F32),
            pltpu.VMEM((16, count * size), F32),
            dma((5,)),
            dma((4,)), dma((2,)), dma((4,)), dma((40,)), dma((40,)), dma((32,)), dma((32,)),
            dma((shards,)), dma((shards,)), dma((shards,)), dma((shards,)), dma((shards,)), dma((shards,)),
            dma((16,)), dma((16,)),
        ],
        compiler_params=pltpu.CompilerParams(
            vmem_limit_bytes=VMEM_LIMIT, collective_id=0, has_side_effects=True
        ),
    )(temper, place, extended, place, level_two, level_three)

    new_centroids = sums.reshape(blocks * size, depth).astype(F32)
    return soft_codes, candidate_scores, new_centroids, cluster_mass.reshape(blocks * size)


def solution(mesh):
    rows = P(("dp", "clus"), None)
    return jax.shard_map(
        body,
        mesh=mesh,
        in_specs=(rows, rows, rows, P("clus"), P("clus", None), P("clus", None)),
        out_specs=(rows, rows, P("clus", None), P("clus")),
        check_vma=False,
    )
```
